32 devices in a mesh: parts: 2 (over y), blk: 16 (over z, x, core).
Axes of the slice: x: 2, y: 2, z: 4, core: 2. Of those that a mesh axis runs over, the one named last changes fastest.
Arguments:
- features: bfloat16 [8192, 128], P(('parts', 'blk')), parts along dimension 0, may hold values from -6 to 6
- w_first: bfloat16 [128, 256], replicated, may hold values from -0.5 to 0.5
- w_second: bfloat16 [256, 8192], replicated, may hold values from -0.375 to 0.375
- panel: bfloat16 [64, 64, 256], P(('parts', 'blk')), parts along dimension 0, may hold values from -6 to 6
- energies: float32 [256], replicated, may hold values from -1 to 1
- pair_dest: int32 [8192, 1], P(('parts', 'blk')), parts along dimension 0, may hold values from 0 to 15, as said below
- pair_row: int32 [8192], P(('parts', 'blk')), parts along dimension 0, may hold values from 0 to 1
- pair_col: int32 [8192], P(('parts', 'blk')), parts along dimension 0, may hold values from 0 to 1
Outputs:
- residual: float32 [64, 64, 256], P(('parts', 'blk')), parts along dimension 0
- loss: float32 [2], P('parts'), parts along dimension 0
- grad_first: float32 [256, 256], P('parts'), parts along dimension 0
- grad_second: float32 [512, 8192], P('parts', 'blk'), parts along dimension 0
The draws below stay inside these ranges and needn't reach their ends.
There are 2 independent parts, one for each index of `parts`. The reference program is written for one: setup_inputs(seed, part) draws one part's arguments, and reference() takes and returns one part's arrays. A program takes and returns all parts, laid end to end along the dimension named above; an argument that names none is the same for every part. Nothing has to cross between parts.
Inputs may be any that keep to these rules, and one draw needn't show every extreme that they name: `pair_dest`: among one device's 256 pairs at most 24 have their block row on one device; every device owns the block rows of exactly 24 of its own pairs. Owners lie mostly near the listing device along the axis.
All inputs are finite; a program needn't handle non-finite values.
Results may differ from the reference program's by a relative error of at most 0.004.
Values may be sent and summed in bfloat16 or wider, within the bound.
No kernel may reach another device: no remote copies, remote signals or barrier semaphores. Data moves between devices by JAX's collectives and lax.ppermute only.
A program may use at most 128 MiB of HBM per device.

```python
import jax
import jax.numpy as jnp
from jax import lax

O = 64
P_SIZE = 256
F = 128
HID = 256
BLK_DEV = 2
PAIR_DEV = 256
NB = 32
PAIRS = 4096
N_BLK = 16


def draw_pair_dest(key, part):
    count_dev = N_BLK
    per_owner = 3 * PAIR_DEV // (2 * N_BLK)
    offsets = jnp.arange(count_dev, dtype=jnp.int32) - count_dev // 4
    spread = jnp.abs(offsets)
    slot_offset = jnp.repeat(offsets, per_owner, total_repeat_length=count_dev * per_owner)
    slot_spread = jnp.repeat(spread, per_owner, total_repeat_length=count_dev * per_owner)
    slot_total = count_dev * per_owner
    base_key = jax.random.fold_in(key, 7)

    def one_device(device):
        dev_key = jax.random.fold_in(base_key, device)
        first_key, second_key = jax.random.split(dev_key)
        raw = jax.random.randint(first_key, (slot_total,), 0, 4096, dtype=jnp.int32)
        base = jnp.where(slot_spread == 0, jnp.int32(8192), raw // (1 + slot_spread))
        score = base * slot_total + jnp.arange(slot_total, dtype=jnp.int32)
        unused_top, picked = lax.top_k(score, PAIR_DEV)
        chosen = slot_offset[picked]
        chosen = jax.random.permutation(second_key, chosen)
        return jnp.mod(device + chosen, count_dev).astype(jnp.int32)
    owners = jax.vmap(one_device)(jnp.arange(count_dev, dtype=jnp.int32))
    return owners.reshape(count_dev * PAIR_DEV, 1).astype(jnp.int32)


def place_ends(entries, rng, low, top_value):
    extent = entries.shape
    place = [jax.random.randint(jax.random.fold_in(rng, axis), (), 0, extent[axis]) for axis in range(len(extent))]
    entries = entries.at[tuple(place)].set(low)
    longest = extent.index(max(extent))
    place[longest] = (place[longest] + 1) % extent[longest]
    return entries.at[tuple(place)].set(top_value)


def block_scale(rng, shape, shards, smallest, top_value):
    def one(dim, blocks):
        steps = jax.random.uniform(jax.random.fold_in(jax.random.fold_in(rng, 6), dim), (blocks,), jnp.float32, smallest / len(shards), top_value / len(shards))
        return jnp.repeat(jnp.exp(steps), shape[dim] // blocks).reshape((-1,) + (1,) * (len(shape) - dim - 1))

    level = one(*shards[0])
    for cut in shards[1:]:
        level = level * one(*cut)
    return level


def normal_values(stream_key, extent, deviation, limit, cuts=(), kind=jnp.bfloat16):
    result = deviation * jax.random.normal(stream_key, extent, jnp.float32)
    if cuts:
        result = result * block_scale(stream_key, extent, cuts, -0.22, 0.18)
    return jnp.clip(result, -limit, limit).astype(kind)


def setup_inputs(seed: int = 0, part: int = 0) -> dict:
    seeds = jax.random.split(jax.random.key(seed), 9)
    part_splits = jax.random.split(jax.random.fold_in(seeds[8], part), 9)
    features = normal_values(part_splits[0], (PAIRS, F), 1.0, 6.0, ((0, 16),))
    w_first = normal_values(seeds[1], (F, HID), F ** -0.5, 0.5)
    w_second = normal_values(seeds[2], (HID, 2 * O * O), HID ** -0.5, 0.375)
    panel = normal_values(part_splits[3], (NB, O, P_SIZE), 1.0, 6.0, ((0, 16),))
    energies = jnp.clip(jax.random.uniform(seeds[4], (P_SIZE,), jnp.float32, -1.0, 1.0), -1.0, 1.0)
    pair_dest = draw_pair_dest(jax.random.fold_in(jax.random.fold_in(seeds[8], part), 71), part)
    pair_row = place_ends(jax.random.randint(part_splits[6], (PAIRS,), 0, BLK_DEV), jax.random.fold_in(part_splits[6], 1), 0, BLK_DEV - 1).astype(jnp.int32)
    pair_col = place_ends(jax.random.randint(part_splits[7], (PAIRS,), 0, BLK_DEV), jax.random.fold_in(part_splits[7], 1), 0, BLK_DEV - 1).astype(jnp.int32)
    return {"features": features, "w_first": w_first, "w_second": w_second, "panel": panel, "energies": energies, "pair_dest": pair_dest, "pair_row": pair_row, "pair_col": pair_col}


def predict(feats, w_first, w_second):
    pre = jnp.dot(feats, w_first, preferred_element_type=jnp.float32)
    hidden = jax.nn.silu(pre).astype(jnp.bfloat16)
    blocks = (jnp.dot(hidden, w_second, preferred_element_type=jnp.float32) / O).astype(jnp.bfloat16)
    return pre, hidden, blocks


def reference(features, w_first, w_second, panel, energies, pair_dest, pair_row, pair_col):
    total_blocks = BLK_DEV * N_BLK
    devices = jnp.arange(N_BLK, dtype=jnp.int32)
    feats_dev = features.reshape(N_BLK, PAIR_DEV, F)
    dest_dev = pair_dest[:, 0].reshape(N_BLK, PAIR_DEV).astype(jnp.int32)
    row_dev = pair_row.reshape(N_BLK, PAIR_DEV).astype(jnp.int32)
    col_dev = pair_col.reshape(N_BLK, PAIR_DEV).astype(jnp.int32)
    items = (devices, feats_dev, dest_dev, row_dev, col_dev)

    def forward(total, item):
        device, feats, dest, prow, pcol = item
        row_glob = (dest * BLK_DEV + prow).astype(jnp.int32)
        col_glob = (device * BLK_DEV + pcol).astype(jnp.int32)
        unused_pre, unused_hidden, blocks = predict(feats, w_first, w_second)
        blocks = blocks.reshape(PAIR_DEV, 2, O, O).astype(jnp.float32)
        coeffs = panel[col_glob].astype(jnp.float32)
        h_panel = jnp.einsum('sab,sbp->sap', blocks[:, 0], coeffs, precision=lax.Precision.HIGHEST)
        s_panel = jnp.einsum('sab,sbp->sap', blocks[:, 1], coeffs, precision=lax.Precision.HIGHEST)
        contrib = h_panel - s_panel * energies
        return total.at[row_glob].add(contrib), None

    residual = lax.scan(forward, jnp.zeros((total_blocks, O, P_SIZE), jnp.float32), items)[0]
    loss = (jnp.sum(residual * residual) / (total_blocks * O * P_SIZE)).reshape(1)
    grad_h = (residual / total_blocks).astype(jnp.bfloat16)
    grad_s = (-(residual * energies) / total_blocks).astype(jnp.bfloat16)

    def backward(carry, item):
        acc_first, acc_second = carry
        device, feats, dest, prow, pcol = item
        row_glob = (dest * BLK_DEV + prow).astype(jnp.int32)
        col_glob = (device * BLK_DEV + pcol).astype(jnp.int32)
        pre, hidden, unused_blocks = predict(feats, w_first, w_second)
        coeffs = panel[col_glob].astype(jnp.float32)
        gh_rows = grad_h[row_glob].astype(jnp.float32)
        gs_rows = grad_s[row_glob].astype(jnp.float32)
        d_h = jnp.einsum('sap,sbp->sab', gh_rows, coeffs, precision=lax.Precision.HIGHEST).astype(jnp.bfloat16)
        d_s = jnp.einsum('sap,sbp->sab', gs_rows, coeffs, precision=lax.Precision.HIGHEST).astype(jnp.bfloat16)
        d_flat = jnp.stack([d_h, d_s], axis=1).reshape(PAIR_DEV, 2 * O * O)
        acc_second = acc_second + jnp.dot(hidden.T, d_flat, preferred_element_type=jnp.float32) / O
        d_hidden = jnp.dot(d_flat, w_second.T, preferred_element_type=jnp.float32) / O
        sig = jax.nn.sigmoid(pre)
        d_pre = (d_hidden * sig * (1.0 + pre * (1.0 - sig))).astype(jnp.bfloat16)
        acc_first = acc_first + jnp.dot(feats.T, d_pre, preferred_element_type=jnp.float32)
        return (acc_first, acc_second), None

    start = (jnp.zeros((F, HID), jnp.float32), jnp.zeros((HID, 2 * O * O), jnp.float32))
    grad_first, grad_second = lax.scan(backward, start, items)[0]
    return (residual, loss, grad_first, grad_second)
```

```python
import functools

import jax
import jax.numpy as jnp
from jax import lax
from jax.experimental import pallas as pl
from jax.experimental.pallas import tpu as pltpu
from jax.sharding import PartitionSpec as P

BF16 = jnp.bfloat16
F32 = jnp.float32
VMEM_LIMIT = 56 << 20


def dot(a, b, dims):
    return lax.dot_general(a, b, ((dims[:1], dims[1:]), ((), ())), preferred_element_type=F32)


def group_kernel(gid_ref, feats_ref, w_first_ref, out_ref, *, orbitals):
    pre = dot(feats_ref[...], w_first_ref[...], (1, 0))
    hidden = (pre / (1.0 + jnp.exp(-pre))).astype(BF16)
    groups, pairs = out_ref.shape[0], feats_ref.shape[0]
    rows = lax.broadcasted_iota(jnp.int32, (groups, pairs), 0)
    pick = (rows == gid_ref[...]).astype(F32).astype(BF16)
    out_ref[...] = (dot(pick, hidden, (1, 0)) * (1.0 / orbitals)).astype(BF16)


def swap_kernel(w_ref, out_ref):
    for k in range(w_ref.shape[1] // 128):
        cols = slice(k * 128, (k + 1) * 128)
        out_ref[:, cols] = pltpu.roll(w_ref[:, cols].astype(F32), 64, 1).astype(BF16)


def main_kernel(*refs, chips, z_count, rows_split, half_cols):
    (me_ref, *piece_refs) = refs[: 1 + chips]
    (
        partner_ref,
        feats_ref,
        gid_ref,
        w_first_ref,
        w_ref,
        w_swap_ref,
        energies_ref,
        res_ref,
        keep_ref,
        send_ref,
        first_ref,
        h_ref,
        c_ref,
        x_ref,
        r_ref,
        g_ref,
        l_ref,
        dh_ref,
    ) = refs[1 + chips :]
    me = me_ref[0]
    core = me % 2
    chip = me // 2
    x_count = chips // z_count
    my_z, my_x = chip // x_count, chip % x_count
    listers = 2 * chips
    rs = rows_split
    hid = w_ref.shape[0]
    half = w_ref.shape[1] // 2
    columns = energies_ref.shape[1]
    ah_count = half // 128
    total_blocks = 2 * rs
    lane = lax.broadcasted_iota(jnp.int32, (rs, 128), 1)
    low = lane < 64

    def place(lister, block):
        at = pl.multiple_of(lister * 128, 128)
        c_ref[0, pl.ds(at, 128), :] = block
        c_ref[1, pl.ds(at, 64), :] = block[64:, :]
        c_ref[1, pl.ds(at + 64, 64), :] = block[:64, :]

    for m in range(chips):
        dz, dx = m // x_count, m % x_count
        src = ((my_z - dz) % z_count) * x_count + (my_x - dx) % x_count
        same, other = 2 * src + core, 2 * src + 1 - core
        piece = piece_refs[m]
        place(same, piece[4 * rs : 4 * rs + 128, :])
        place(other, partner_ref[m * 128 : (m + 1) * 128, :])
        for which, lister in ((0, same), (1, other)):
            at = pl.multiple_of(lister * rs, rs)
            for pc in range(2):
                lo = which * 2 * rs + pc * rs
                h_ref[pc, pl.ds(at, rs), :] = piece[lo : lo + rs, :]

    h0, h1 = h_ref[0], h_ref[1]
    step_cols = 512
    steps = half // step_cols
    per = step_cols // 128

    def forward(i, carry):
        hs, nb = i // steps, i % steps
        at = pl.multiple_of(i * step_cols, step_cols)
        y0 = dot(h0, w_ref[:, pl.ds(at, step_cols)], (1, 0))
        y1 = dot(h1, w_swap_ref[:, pl.ds(at, step_cols)], (1, 0))
        for k in range(per):
            row = pl.multiple_of((hs * ah_count + nb * per + k) * rs, rs)
            for j in range(listers):
                v0 = y0[j * rs : (j + 1) * rs, k * 128 : (k + 1) * 128]
                v1 = y1[j * rs : (j + 1) * rs, k * 128 : (k + 1) * 128]
                cols = slice(j * 128, (j + 1) * 128)
                x_ref[0, pl.ds(row, rs), cols] = jnp.where(low, v0, v1).astype(BF16)
                x_ref[1, pl.ds(row, rs), cols] = jnp.where(low, v1, v0).astype(BF16)
        return carry

    lax.fori_loop(0, 2 * steps, forward, 0)

    energies = energies_ref[...]
    n_rows = ah_count * rs
    mb = 256
    f_width = w_first_ref.shape[0]
    first_ref[...] = jnp.zeros_like(first_ref)

    def product(i, carry):
        par, b = i // (n_rows // mb), i % (n_rows // mb)
        at = pl.multiple_of(b * mb, mb)
        r_h = dot(x_ref[par, pl.ds(at, mb), :], c_ref[par], (1, 0))
        r_s = dot(x_ref[par, pl.ds(n_rows + at, mb), :], c_ref[par], (1, 0))
        res = r_h - r_s * energies
        r_ref[par, pl.ds(at, mb), :] = res
        g_ref[0, par, pl.ds(at, mb), :] = (res / total_blocks).astype(BF16)
        g_ref[1, par, pl.ds(at, mb), :] = (-(res * energies) / total_blocks).astype(BF16)
        first_ref[f_width:, :] += jnp.sum((res * res).reshape(mb // 8, 8, columns), axis=0)
        return carry

    lax.fori_loop(0, 2 * (n_rows // mb), product, 0)

    blk_dev = res_ref.shape[0]
    for i in range(blk_dev):
        for par in range(2):
            for ah in range(ah_count):
                res_ref[i, 2 * ah + par : 2 * ah + par + 1, :] = r_ref[
                    par, pl.ds(ah * rs + chip * blk_dev + i, 1), :
                ]

    jb_count = 2
    jb_width = jb_count * 128

    def backward(i, carry):
        hs, jb = i // (listers // jb_count), i % (listers // jb_count)
        at = pl.multiple_of(jb * jb_width, jb_width)
        d_e = dot(g_ref[hs, 0], c_ref[0, pl.ds(at, jb_width), :], (1, 1))
        d_o = dot(g_ref[hs, 1], c_ref[1, pl.ds(at, jb_width), :], (1, 1))
        for j in range(jb_count):
            row = pl.multiple_of((jb * jb_count + j) * rs, rs)
            for ah in range(ah_count):
                v0 = d_e[ah * rs : (ah + 1) * rs, j * 128 : (j + 1) * 128]
                v1 = d_o[ah * rs : (ah + 1) * rs, j * 128 : (j + 1) * 128]
                cols = pl.ds(pl.multiple_of(hs * half + ah * 128, 128), 128)
                l_ref[0, pl.ds(row, rs), cols] = jnp.where(low, v0, v1).astype(BF16)
                l_ref[1, pl.ds(row, rs), cols] = jnp.where(low, v1, v0).astype(BF16)
        return carry

    lax.fori_loop(0, 2 * (listers // jb_count), backward, 0)

    orbitals = 64
    for pc, weights in ((0, w_ref), (1, w_swap_ref)):
        dh_ref[pc] = dot(l_ref[pc], weights[...], (1, 1)) / orbitals

    width = 2 * half_cols
    at = pl.multiple_of(chip * width, width)
    g0 = dot(h0, l_ref[0, :, pl.ds(at, width)], (0, 0))
    g1 = dot(h1, l_ref[1, :, pl.ds(at, width)], (0, 0))
    even = core == 0
    for k in range(half_cols // 128):
        a, b = slice(k * 128, (k + 1) * 128), slice(half_cols + k * 128, half_cols + (k + 1) * 128)
        va = g0[:, a] + pltpu.roll(g1[:, a], 64, 1)
        vb = g0[:, b] + pltpu.roll(g1[:, b], 64, 1)
        keep_ref[:, a] = jnp.where(even, va, vb)
        send_ref[:, a] = jnp.where(even, vb, va)

    pairs = gid_ref.shape[1]
    group_row = lax.broadcasted_iota(jnp.int32, (2 * rs, pairs), 0) + core * (2 * rs)

    def first(j, carry):
        feats = feats_ref[pl.ds(pl.multiple_of(j * pairs, pairs), pairs), :]
        pre = dot(feats, w_first_ref[...], (1, 0))
        sig = 1.0 / (1.0 + jnp.exp(-pre))
        at = pl.multiple_of(j * rs, rs)
        d_group = jnp.concatenate([dh_ref[0, pl.ds(at, rs), :], dh_ref[1, pl.ds(at, rs), :]], axis=0)
        head = d_group.astype(BF16)
        tail = (d_group - head.astype(F32)).astype(BF16)
        pick = (group_row == gid_ref[pl.ds(j, 1), :]).astype(F32).astype(BF16)
        both = jnp.concatenate([head, tail], axis=0)
        d_hidden = dot(jnp.concatenate([pick, pick], axis=0), both, (0, 0))
        d_pre = (d_hidden * sig * (1.0 + pre * (1.0 - sig))).astype(BF16)
        first_ref[:f_width, :] += dot(feats, d_pre, (0, 0))
        return carry

    lax.fori_loop(0, listers, first, 0)


def near(features, w_first, w_second, panel, energies, pair_dest, pair_row, pair_col, z_count):
    n_dev = lax.axis_size("blk")
    me = lax.axis_index("blk")
    pairs, f_width = features.shape
    blk_dev, orbitals, columns = panel.shape
    hid, flat = w_second.shape
    chips, rs = n_dev // 2, n_dev * blk_dev // 2
    x_count = chips // z_count
    half_cols = flat // n_dev
    dest = pair_dest[:, 0]
    gid = (dest % 2) * (2 * rs) + pair_col * rs + (dest // 2) * blk_dev + pair_row

    grouped = pl.pallas_call(
        functools.partial(group_kernel, orbitals=orbitals),
        out_shape=jax.ShapeDtypeStruct((4 * rs, hid), BF16),
        name="group",
    )(gid.reshape(1, pairs), features, w_first)
    w_swap = pl.pallas_call(
        swap_kernel,
        out_shape=jax.ShapeDtypeStruct(w_second.shape, BF16),
        compiler_params=pltpu.CompilerParams(vmem_limit_bytes=VMEM_LIMIT),
        name="swap",
    )(w_second)

    def to_core(v):
        return lax.ppermute(v, "blk", [(i, i ^ 1) for i in range(n_dev)])

    def shift(m):
        dz, dx = m // x_count, m % x_count
        moves = []
        for i in range(n_dev):
            chip, core = i // 2, i % 2
            z, x = chip // x_count, chip % x_count
            to = ((z + dz) % z_count) * x_count + (x + dx) % x_count
            moves.append((i, 2 * to + core))
        return moves

    core = me % 2
    mine = lax.dynamic_slice_in_dim(grouped, core * 2 * rs, 2 * rs, 0)
    theirs = lax.dynamic_slice_in_dim(grouped, (1 - core) * 2 * rs, 2 * rs, 0)
    from_core = to_core(theirs)
    piece = jnp.concatenate([mine, from_core, panel.reshape(blk_dev * orbitals, columns)], axis=0)
    pieces = [piece] + [lax.ppermute(piece, "blk", shift(m)) for m in range(1, chips)]
    partner = to_core(jnp.concatenate([v[4 * rs :] for v in pieces], axis=0))

    pack = jnp.concatenate([features, gid.astype(BF16).reshape(pairs // f_width, f_width)], axis=0)
    packs = jnp.stack([pack] + [lax.ppermute(pack, "blk", shift(m)) for m in range(1, chips)])
    packs = jnp.stack([packs, to_core(packs)], axis=1)
    zz, xx = jnp.meshgrid(jnp.arange(z_count), jnp.arange(x_count), indexing="ij")
    chip = me // 2
    source = ((chip // x_count - zz) % z_count * x_count + (chip % x_count - xx) % x_count).reshape(-1)
    order = jnp.stack([source, source], axis=1) * 2 + jnp.stack([core, 1 - core])[None, :]
    back = jnp.zeros((n_dev,), jnp.int32).at[order.reshape(-1)].set(jnp.arange(n_dev))
    packs = packs.reshape(n_dev, -1, f_width)[back]
    all_feats = packs[:, :pairs].reshape(n_dev * pairs, f_width)
    all_gid = packs[:, pairs:].reshape(n_dev, pairs).astype(jnp.int32)

    listers = n_dev
    k_width = listers * 128
    n_rows = rs * orbitals // 2
    res, keep, send, first = pl.pallas_call(
        functools.partial(main_kernel, chips=chips, z_count=z_count, rows_split=rs, half_cols=half_cols),
        out_shape=(
            jax.ShapeDtypeStruct((blk_dev, orbitals, columns), F32),
            jax.ShapeDtypeStruct((hid, half_cols), F32),
            jax.ShapeDtypeStruct((hid, half_cols), F32),
            jax.ShapeDtypeStruct((f_width + 8, hid), F32),
        ),
        in_specs=[pl.BlockSpec(memory_space=pltpu.SMEM)] + [pl.BlockSpec(memory_space=pltpu.VMEM)] * (chips + 7),
        scratch_shapes=[
            pltpu.VMEM((2, listers * rs, hid), BF16),
            pltpu.VMEM((2, k_width, columns), BF16),
            pltpu.VMEM((2, 2 * n_rows, k_width), BF16),
            pltpu.VMEM((2, n_rows, columns), F32),
            pltpu.VMEM((2, 2, n_rows, columns), BF16),
            pltpu.VMEM((2, listers * rs, flat), BF16),
            pltpu.VMEM((2, listers * rs, hid), F32),
        ],
        compiler_params=pltpu.CompilerParams(vmem_limit_bytes=VMEM_LIMIT),
        name="step",
    )(
        me.reshape(1).astype(jnp.int32),
        *pieces,
        partner,
        all_feats,
        all_gid,
        w_first,
        w_second,
        w_swap,
        energies.reshape(1, columns),
    )
    grad_second = keep + to_core(send)
    first = first + to_core(first)
    loss = (jnp.sum(first[f_width:]) / (n_dev * blk_dev * orbitals * columns)).reshape(1)
    return (res, loss, first[:f_width], grad_second)


def predict(feats, w_first, w_second, orbitals):
    pre = jnp.dot(feats, w_first, preferred_element_type=jnp.float32)
    hidden = jax.nn.silu(pre).astype(jnp.bfloat16)
    blocks = (jnp.dot(hidden, w_second, preferred_element_type=jnp.float32) / orbitals).astype(
        jnp.bfloat16
    )
    return (pre, hidden, blocks)


def weight_terms(feats, pre, hidden, d_flat, w_second, orbitals):
    term_second = jnp.dot(hidden.T, d_flat, preferred_element_type=jnp.float32) / orbitals
    d_hidden = (
        lax.dot_general(
            d_flat, w_second, (((1,), (1,)), ((), ())), preferred_element_type=jnp.float32
        )
        / orbitals
    )
    sig = jax.nn.sigmoid(pre)
    d_pre = (d_hidden * sig * (1.0 + pre * (1.0 - sig))).astype(jnp.bfloat16)
    term_first = jnp.dot(feats.T, d_pre, preferred_element_type=jnp.float32)
    return (term_first, term_second)


def slot_work(slot_blocks, slot_panel, slot_rows, energies, blk_dev, total_blocks):
    slots, unused_two, orbitals, unused_o = slot_blocks.shape
    columns = slot_panel.shape[2]
    group = 32
    steps_count = slots // group
    grouped = (
        slot_blocks.reshape(steps_count, group, 2, orbitals, orbitals),
        slot_panel.reshape(steps_count, group, orbitals, columns),
        slot_rows.reshape(steps_count, group),
    )
    row_ids = jnp.arange(blk_dev, dtype=jnp.int32)

    def forward(total, item):
        blocks, coeffs, rows = item
        h_panel = jnp.einsum(
            "sab,sbp->sap", blocks[:, 0], coeffs, preferred_element_type=jnp.float32
        )
        s_panel = jnp.einsum(
            "sab,sbp->sap", blocks[:, 1], coeffs, preferred_element_type=jnp.float32
        )
        contrib = h_panel - s_panel * energies
        selector = (rows[None, :] == row_ids[:, None]).astype(jnp.float32)
        added = jnp.einsum("rs,sap->rap", selector, contrib, precision=lax.Precision.HIGHEST)
        return (total + added, None)

    residual = lax.scan(forward, jnp.zeros((blk_dev, orbitals, columns), jnp.float32), grouped)[0]
    grad_h = (residual / total_blocks).astype(jnp.bfloat16)
    grad_s = (-(residual * energies) / total_blocks).astype(jnp.bfloat16)

    def backward(carry, item):
        blocks, coeffs, rows = item
        valid = (rows >= 0)[:, None, None]
        safe_rows = jnp.maximum(rows, 0)
        gh_rows = jnp.where(valid, grad_h[safe_rows], jnp.zeros((), jnp.bfloat16))
        gs_rows = jnp.where(valid, grad_s[safe_rows], jnp.zeros((), jnp.bfloat16))
        d_h = jnp.einsum(
            "sap,sbp->sab", gh_rows, coeffs, preferred_element_type=jnp.float32
        ).astype(jnp.bfloat16)
        d_s = jnp.einsum(
            "sap,sbp->sab", gs_rows, coeffs, preferred_element_type=jnp.float32
        ).astype(jnp.bfloat16)
        return (carry, jnp.stack([d_h, d_s], axis=1))

    d_blocks = lax.scan(backward, 0, grouped)[1]
    return (residual, d_blocks.reshape(slots, 2, orbitals, orbitals))


def local(features, w_first, w_second, panel, energies, pair_dest, pair_row, pair_col):
    n_dev = lax.axis_size("blk")
    my_index = lax.axis_index("blk")
    pair_count, feat_width = features.shape
    blk_dev, orbitals, columns = panel.shape
    capacity = 3 * pair_count // (2 * n_dev)
    slots = n_dev * capacity
    total_blocks = blk_dev * n_dev
    dest = pair_dest[:, 0]
    dest_table = (dest[:, None] == jnp.arange(n_dev, dtype=jnp.int32)[None, :]).astype(jnp.int32)
    rank_in = jnp.sum(jnp.cumsum(dest_table, axis=0) * dest_table, axis=1) - 1
    slot_of = dest * capacity + rank_in
    source = (
        jnp.full((slots,), pair_count, jnp.int32)
        .at[slot_of]
        .set(jnp.arange(pair_count, dtype=jnp.int32))
    )
    empty_label = jnp.full((1,), -1, jnp.int32)
    rows_sent = jnp.concatenate([pair_row, empty_label])[source]
    cols_sent = jnp.concatenate([my_index * blk_dev + pair_col, jnp.zeros((1,), jnp.int32)])[source]
    labels = jnp.stack([rows_sent, cols_sent], axis=-1).reshape(n_dev, capacity, 2)
    whole_panel = lax.all_gather(panel, "blk", axis=0, tiled=True)
    pre, hidden, blocks = predict(features, w_first, w_second, orbitals)
    padded = jnp.concatenate([blocks, jnp.zeros((1, blocks.shape[1]), jnp.bfloat16)], axis=0)
    send_blocks = padded[source].reshape(n_dev, capacity, 2, orbitals, orbitals)
    got_blocks, got_labels = (
        lax.all_to_all(send_blocks, "blk", split_axis=0, concat_axis=0, tiled=True),
        lax.all_to_all(labels, "blk", split_axis=0, concat_axis=0, tiled=True),
    )
    got_labels = got_labels.reshape(slots, 2)
    slot_panel = whole_panel[got_labels[:, 1]]
    residual, d_blocks = slot_work(
        got_blocks.reshape(slots, 2, orbitals, orbitals),
        slot_panel,
        got_labels[:, 0],
        energies,
        blk_dev,
        total_blocks,
    )
    back = lax.all_to_all(
        d_blocks.reshape(n_dev, capacity, 2, orbitals, orbitals),
        "blk",
        split_axis=0,
        concat_axis=0,
        tiled=True,
    )
    d_flat = back.reshape(slots, 2 * orbitals * orbitals)[slot_of]
    term_first, term_second = weight_terms(features, pre, hidden, d_flat, w_second, orbitals)
    grad_second = lax.psum_scatter(term_second, "blk", scatter_dimension=1, tiled=True)
    grad_first, square_sum = lax.psum((term_first, jnp.sum(residual * residual)), "blk")
    loss = (square_sum / (total_blocks * orbitals * columns)).reshape(1)
    return (residual, loss, grad_first, grad_second)


def solution(mesh):
    in_specs = (
        P(("parts", "blk"), None),
        P(),
        P(),
        P(("parts", "blk"), None, None),
        P(),
        P(("parts", "blk"), None),
        P(("parts", "blk")),
        P(("parts", "blk")),
    )
    out_specs = (P(("parts", "blk"), None, None), P("parts"), P("parts", None), P("parts", "blk"))
    n_dev = mesh.shape["blk"]
    step = functools.partial(near, z_count=4) if n_dev == 16 else local
    return jax.shard_map(step, mesh=mesh, in_specs=in_specs, out_specs=out_specs, check_vma=False)
```

```python
import functools

import jax
import jax.numpy as jnp
from jax import lax
from jax.experimental import pallas as pl
from jax.experimental.pallas import tpu as pltpu
from jax.sharding import PartitionSpec as P

BF16 = jnp.bfloat16
F32 = jnp.float32
MAIN_VMEM = 36 << 20
WEIGHTS_VMEM = 10 << 20
X_AFTER = 5


def dot(a, b, dims):
    return lax.dot_general(a, b, ((dims[:1], dims[1:]), ((), ())), preferred_element_type=F32)


def group_kernel(dest_ref, row_ref, col_ref, feats_ref, w_first_ref, panel_ref, piece_ref, *, rs, blk_dev, orbitals):
    pre = dot(feats_ref[...], w_first_ref[...], (1, 0))
    hidden = (pre * (0.5 * jnp.tanh(0.5 * pre) + 0.5)).astype(BF16)
    pairs = feats_ref.shape[0]
    dest = dest_ref[...]
    gid = (dest % 2) * (2 * rs) + col_ref[...] * rs + (dest // 2) * blk_dev + row_ref[...]
    rows = lax.broadcasted_iota(jnp.int32, (4 * rs, pairs), 0)
    pick = (rows == gid).astype(F32).astype(BF16)
    panel_end = 4 * rs + panel_ref.shape[0]
    piece_ref[: 4 * rs, :] = (dot(pick, hidden, (1, 0)) * (1.0 / orbitals)).astype(BF16)
    piece_ref[4 * rs : panel_end, :] = panel_ref[...]
    piece_ref[panel_end:, :] = jnp.broadcast_to(gid.astype(F32), (8, pairs)).astype(BF16)


def weights_kernel(w_ref, out_ref, sems):
    chunks = sems.shape[0]
    width = w_ref.shape[1] // chunks
    copies = []
    for k in range(chunks):
        cols = slice(k * width, (k + 1) * width)
        copies.append(pltpu.make_async_copy(w_ref.at[:, cols], out_ref.at[0, :, cols], sems.at[k]))
        copies[-1].start()
    for k in range(chunks):
        copies[k].wait()
        for q in range(k * width // 128, (k + 1) * width // 128):
            cols = slice(q * 128, (q + 1) * 128)
            out_ref[1, :, cols] = pltpu.roll(out_ref[0, :, cols].astype(F32), 64, 1).astype(BF16)


def source_chip(m, chip, chips, z_count):
    x_count = chips // z_count
    return ((chip // x_count - m // x_count) % z_count) * x_count + (chip % x_count - m % x_count) % x_count


def main_kernel(*refs, chips, z_count, rows_split, half_cols, orbitals):
    me_ref, same_refs, other_refs = refs[0], refs[1 : 1 + chips], refs[1 + chips : 1 + 2 * chips]
    (w_ref, energies_ref, res_ref, keep_ref, send_ref, dh_ref, square_ref, h_ref, c_ref, x_ref, r_ref, g_ref, l_ref) = refs[
        1 + 2 * chips :
    ]
    me = me_ref[0]
    core = me % 2
    chip = me // 2
    listers = 2 * chips
    rs = rows_split
    half = w_ref.shape[2] // 2
    columns = energies_ref.shape[1]
    ah_count = half // 128
    total_blocks = 2 * rs
    lane = lax.broadcasted_iota(jnp.int32, (rs, 128), 1)
    low = lane < 64

    def place(lister, block):
        at = pl.multiple_of(lister * 128, 128)
        c_ref[0, pl.ds(at, 128), :] = block
        c_ref[1, pl.ds(at, 64), :] = block[64:, :]
        c_ref[1, pl.ds(at + 64, 64), :] = block[:64, :]

    for m in range(chips):
        src = source_chip(m, chip, chips, z_count)
        for piece, lister in ((same_refs[m], 2 * src + core), (other_refs[m], 2 * src + 1 - core)):
            place(lister, piece[4 * rs : 4 * rs + 128, :])
            at = pl.multiple_of(lister * rs, rs)
            for pc in range(2):
                h_ref[pc, pl.ds(at, rs), :] = piece[pl.ds(pl.multiple_of(core * 2 * rs, rs) + pc * rs, rs), :]

    h0, h1 = h_ref[0], h_ref[1]
    step_cols = 2048
    steps = half // step_cols
    per = step_cols // 128

    def forward(i, carry):
        hs, nb = i // steps, i % steps
        at = pl.multiple_of(i * step_cols, step_cols)
        y0 = dot(h0, w_ref[0, :, pl.ds(at, step_cols)], (1, 0))
        y1 = dot(h1, w_ref[1, :, pl.ds(at, step_cols)], (1, 0))
        for k in range(per):
            row = pl.multiple_of((hs * ah_count + nb * per + k) * rs, rs)
            for j in range(listers):
                v0 = y0[j * rs : (j + 1) * rs, k * 128 : (k + 1) * 128]
                v1 = y1[j * rs : (j + 1) * rs, k * 128 : (k + 1) * 128]
                cols = slice(j * 128, (j + 1) * 128)
                x_ref[0, pl.ds(row, rs), cols] = jnp.where(low, v0, v1).astype(BF16)
                x_ref[1, pl.ds(row, rs), cols] = jnp.where(low, v1, v0).astype(BF16)
        return carry

    lax.fori_loop(0, 2 * steps, forward, 0)

    energies = energies_ref[...]
    n_rows = ah_count * rs
    mb = 512
    square_ref[...] = jnp.zeros_like(square_ref)

    def product(i, carry):
        par, b = i // (n_rows // mb), i % (n_rows // mb)
        at = pl.multiple_of(b * mb, mb)
        r_h = dot(x_ref[par, pl.ds(at, mb), :], c_ref[par], (1, 0))
        r_s = dot(x_ref[par, pl.ds(n_rows + at, mb), :], c_ref[par], (1, 0))
        res = r_h - r_s * energies
        r_ref[par, pl.ds(at, mb), :] = res
        g_ref[0, par, pl.ds(at, mb), :] = (res / total_blocks).astype(BF16)
        g_ref[1, par, pl.ds(at, mb), :] = (-(res * energies) / total_blocks).astype(BF16)
        square_ref[...] += jnp.sum((res * res).reshape(mb // 8, 8, columns), axis=0)
        return carry

    lax.fori_loop(0, 2 * (n_rows // mb), product, 0)

    blk_dev = res_ref.shape[0]
    for i in range(blk_dev):
        for par in range(2):
            for ah in range(ah_count):
                res_ref[i, 2 * ah + par : 2 * ah + par + 1, :] = r_ref[
                    par, pl.ds(ah * rs + chip * blk_dev + i, 1), :
                ]

    jb_count = 8
    jb_width = jb_count * 128

    def backward(i, carry):
        hs, jb = i // (listers // jb_count), i % (listers // jb_count)
        at = pl.multiple_of(jb * jb_width, jb_width)
        d_e = dot(g_ref[hs, 0], c_ref[0, pl.ds(at, jb_width), :], (1, 1))
        d_o = dot(g_ref[hs, 1], c_ref[1, pl.ds(at, jb_width), :], (1, 1))
        for j in range(jb_count):
            row = pl.multiple_of((jb * jb_count + j) * rs, rs)
            for ah in range(ah_count):
                v0 = d_e[ah * rs : (ah + 1) * rs, j * 128 : (j + 1) * 128]
                v1 = d_o[ah * rs : (ah + 1) * rs, j * 128 : (j + 1) * 128]
                cols = pl.ds(pl.multiple_of(hs * half + ah * 128, 128), 128)
                l_ref[0, pl.ds(row, rs), cols] = jnp.where(low, v0, v1).astype(BF16)
                l_ref[1, pl.ds(row, rs), cols] = jnp.where(low, v1, v0).astype(BF16)
        return carry

    lax.fori_loop(0, 2 * (listers // jb_count), backward, 0)

    for pc in range(2):
        dh_ref[pc] = dot(l_ref[pc], w_ref[pc], (1, 1)) / orbitals

    width = 2 * half_cols
    at = pl.multiple_of(chip * width, width)
    g0 = dot(h0, l_ref[0, :, pl.ds(at, width)], (0, 0))
    g1 = dot(h1, l_ref[1, :, pl.ds(at, width)], (0, 0))
    even = core == 0
    for k in range(half_cols // 128):
        a, b = slice(k * 128, (k + 1) * 128), slice(half_cols + k * 128, half_cols + (k + 1) * 128)
        va = g0[:, a] + pltpu.roll(g1[:, a], 64, 1)
        vb = g0[:, b] + pltpu.roll(g1[:, b], 64, 1)
        keep_ref[:, a] = jnp.where(even, va, vb)
        send_ref[:, a] = jnp.where(even, vb, va)


def first_kernel(*refs, chips, z_count, rs, pairs):
    me_ref, same_refs, other_refs = refs[0], refs[1 : 1 + chips], refs[1 + chips : 1 + 2 * chips]
    feat_refs = refs[1 + 2 * chips : 5 + 2 * chips]
    w_first_ref, dh_ref, square_ref, first_ref, f_ref, d_ref = refs[5 + 2 * chips :]
    me = me_ref[0]
    core, chip = me % 2, me // 2
    f_width = w_first_ref.shape[0]
    x_count = chips // z_count
    group_row = (lax.broadcasted_iota(jnp.int32, (2 * rs, pairs), 0) + core * (2 * rs)).astype(F32)
    for m in range(chips):
        src = source_chip(m, chip, chips, z_count)
        dz, dx = m // x_count, m % x_count
        for which, (piece, lister) in enumerate(((same_refs[m], 2 * src + core), (other_refs[m], 2 * src + 1 - core))):
            feats = feat_refs[2 * which + dx][dz * pairs : (dz + 1) * pairs, :]
            label = piece[piece.shape[0] - 8 :, :].astype(F32)[:1, :]
            pre = dot(feats, w_first_ref[...], (1, 0))
            sig = 0.5 * jnp.tanh(0.5 * pre) + 0.5
            at = pl.multiple_of(lister * rs, rs)
            d_group = jnp.concatenate([dh_ref[0, pl.ds(at, rs), :], dh_ref[1, pl.ds(at, rs), :]], axis=0)
            head = d_group.astype(BF16)
            tail = (d_group - head.astype(F32)).astype(BF16)
            both = jnp.concatenate([head, tail], axis=0)
            pick = (group_row == label).astype(F32).astype(BF16)
            d_hidden = dot(jnp.concatenate([pick, pick], axis=0), both, (0, 0))
            to = pl.multiple_of(lister * pairs, pairs)
            d_ref[pl.ds(to, pairs), :] = (d_hidden * sig * (1.0 + pre * (1.0 - sig))).astype(BF16)
            f_ref[pl.ds(to, pairs), :] = feats
    first_ref[:f_width, :] = dot(f_ref[...], d_ref[...], (0, 0))
    first_ref[f_width:, :] = square_ref[...]


def near(features, w_first, w_second, panel, energies, pair_dest, pair_row, pair_col, z_count):
    n_dev = lax.axis_size("blk")
    me = lax.axis_index("blk").reshape(1).astype(jnp.int32)
    pairs, f_width = features.shape
    blk_dev, orbitals, columns = panel.shape
    hid, flat = w_second.shape
    chips, rs = n_dev // 2, n_dev * blk_dev // 2
    half_cols = flat // n_dev
    smem, vmem = pl.BlockSpec(memory_space=pltpu.SMEM), pl.BlockSpec(memory_space=pltpu.VMEM)

    def to_x(v):
        return from_chip(v, 1)

    piece = pl.pallas_call(
        functools.partial(group_kernel, rs=rs, blk_dev=blk_dev, orbitals=orbitals),
        out_shape=jax.ShapeDtypeStruct((4 * rs + blk_dev * orbitals + 8, hid), BF16),
        cost_estimate=pl.CostEstimate(flops=1 << 28, transcendentals=0, bytes_accessed=1 << 20),
        name="group",
    )(
        pair_dest.reshape(1, pairs),
        pair_row.reshape(1, pairs),
        pair_col.reshape(1, pairs),
        features,
        w_first,
        panel.reshape(blk_dev * orbitals, columns),
    )
    weights = pl.pallas_call(
        weights_kernel,
        out_shape=jax.ShapeDtypeStruct((2, hid, flat), BF16),
        in_specs=[pl.BlockSpec(memory_space=pl.ANY)],
        scratch_shapes=[pltpu.SemaphoreType.DMA((8,))],
        compiler_params=pltpu.CompilerParams(vmem_limit_bytes=WEIGHTS_VMEM),
        cost_estimate=pl.CostEstimate(flops=0, transcendentals=0, bytes_accessed=8 * hid * flat),
        name="weights",
    )(w_second)

    def to_core(v):
        return lax.ppermute(v, "blk", [(i, i ^ 1) for i in range(n_dev)])

    def from_chip(v, m):
        sends = [(2 * source_chip(m, q, chips, z_count) + c, 2 * q + c) for q in range(chips) for c in range(2)]
        return lax.ppermute(v, "blk", sends) if m else v

    x_count = chips // z_count
    parts = [from_chip(features, dz * x_count) for dz in range(z_count)]
    piece, *parts = lax.optimization_barrier((piece, *parts))
    same = [from_chip(piece, m) for m in range(chips)]
    feats_mine, same[X_AFTER] = lax.optimization_barrier((jnp.concatenate(parts, axis=0), same[X_AFTER]))
    feats = [feats_mine, to_x(feats_mine)]
    other = [to_core(v) for v in same]
    feats += [to_core(v) for v in feats]

    listers = n_dev
    k_width = listers * 128
    n_rows = rs * orbitals // 2
    res, keep, send, d_hidden, square = pl.pallas_call(
        functools.partial(
            main_kernel, chips=chips, z_count=z_count, rows_split=rs, half_cols=half_cols, orbitals=orbitals
        ),
        out_shape=(
            jax.ShapeDtypeStruct((blk_dev, orbitals, columns), F32),
            jax.ShapeDtypeStruct((hid, half_cols), F32),
            jax.ShapeDtypeStruct((hid, half_cols), F32),
            jax.ShapeDtypeStruct((2, listers * rs, hid), F32),
            jax.ShapeDtypeStruct((8, columns), F32),
        ),
        in_specs=[smem] + [vmem] * (2 * chips + 2),
        scratch_shapes=[
            pltpu.VMEM((2, listers * rs, hid), BF16),
            pltpu.VMEM((2, k_width, columns), BF16),
            pltpu.VMEM((2, 2 * n_rows, k_width), BF16),
            pltpu.VMEM((2, n_rows, columns), F32),
            pltpu.VMEM((2, 2, n_rows, columns), BF16),
            pltpu.VMEM((2, listers * rs, flat), BF16),
        ],
        compiler_params=pltpu.CompilerParams(vmem_limit_bytes=MAIN_VMEM),
        cost_estimate=pl.CostEstimate(flops=16 * listers * rs * hid * flat, transcendentals=0, bytes_accessed=1 << 24),
        name="step",
    )(me, *same, *other, weights, energies.reshape(1, columns))
    send = to_core(send)
    first = pl.pallas_call(
        functools.partial(first_kernel, chips=chips, z_count=z_count, rs=rs, pairs=pairs),
        out_shape=jax.ShapeDtypeStruct((f_width + 8, hid), F32),
        in_specs=[smem] + [vmem] * (2 * chips + 7),
        scratch_shapes=[pltpu.VMEM((n_dev * pairs, f_width), BF16), pltpu.VMEM((n_dev * pairs, hid), BF16)],
        compiler_params=pltpu.CompilerParams(vmem_limit_bytes=12 << 20),
        cost_estimate=pl.CostEstimate(flops=1 << 31, transcendentals=0, bytes_accessed=1 << 22),
        name="first",
    )(me, *same, *other, *feats, w_first, d_hidden, square)
    grad_second = keep + send
    first = first + to_core(first)
    loss = (jnp.sum(first[f_width:]) / (n_dev * blk_dev * orbitals * columns)).reshape(1)
    return (res, loss, first[:f_width], grad_second)


def predict(feats, w_first, w_second, orbitals):
    pre = jnp.dot(feats, w_first, preferred_element_type=jnp.float32)
    hidden = jax.nn.silu(pre).astype(jnp.bfloat16)
    blocks = (jnp.dot(hidden, w_second, preferred_element_type=jnp.float32) / orbitals).astype(
        jnp.bfloat16
    )
    return (pre, hidden, blocks)


def weight_terms(feats, pre, hidden, d_flat, w_second, orbitals):
    term_second = jnp.dot(hidden.T, d_flat, preferred_element_type=jnp.float32) / orbitals
    d_hidden = (
        lax.dot_general(
            d_flat, w_second, (((1,), (1,)), ((), ())), preferred_element_type=jnp.float32
        )
        / orbitals
    )
    sig = jax.nn.sigmoid(pre)
    d_pre = (d_hidden * sig * (1.0 + pre * (1.0 - sig))).astype(jnp.bfloat16)
    term_first = jnp.dot(feats.T, d_pre, preferred_element_type=jnp.float32)
    return (term_first, term_second)


def slot_work(slot_blocks, slot_panel, slot_rows, energies, blk_dev, total_blocks):
    slots, unused_two, orbitals, unused_o = slot_blocks.shape
    columns = slot_panel.shape[2]
    group = 32
    steps_count = slots // group
    grouped = (
        slot_blocks.reshape(steps_count, group, 2, orbitals, orbitals),
        slot_panel.reshape(steps_count, group, orbitals, columns),
        slot_rows.reshape(steps_count, group),
    )
    row_ids = jnp.arange(blk_dev, dtype=jnp.int32)

    def forward(total, item):
        blocks, coeffs, rows = item
        h_panel = jnp.einsum(
            "sab,sbp->sap", blocks[:, 0], coeffs, preferred_element_type=jnp.float32
        )
        s_panel = jnp.einsum(
            "sab,sbp->sap", blocks[:, 1], coeffs, preferred_element_type=jnp.float32
        )
        contrib = h_panel - s_panel * energies
        selector = (rows[None, :] == row_ids[:, None]).astype(jnp.float32)
        added = jnp.einsum("rs,sap->rap", selector, contrib, precision=lax.Precision.HIGHEST)
        return (total + added, None)

    residual = lax.scan(forward, jnp.zeros((blk_dev, orbitals, columns), jnp.float32), grouped)[0]
    grad_h = (residual / total_blocks).astype(jnp.bfloat16)
    grad_s = (-(residual * energies) / total_blocks).astype(jnp.bfloat16)

    def backward(carry, item):
        blocks, coeffs, rows = item
        valid = (rows >= 0)[:, None, None]
        safe_rows = jnp.maximum(rows, 0)
        gh_rows = jnp.where(valid, grad_h[safe_rows], jnp.zeros((), jnp.bfloat16))
        gs_rows = jnp.where(valid, grad_s[safe_rows], jnp.zeros((), jnp.bfloat16))
        d_h = jnp.einsum(
            "sap,sbp->sab", gh_rows, coeffs, preferred_element_type=jnp.float32
        ).astype(jnp.bfloat16)
        d_s = jnp.einsum(
            "sap,sbp->sab", gs_rows, coeffs, preferred_element_type=jnp.float32
        ).astype(jnp.bfloat16)
        return (carry, jnp.stack([d_h, d_s], axis=1))

    d_blocks = lax.scan(backward, 0, grouped)[1]
    return (residual, d_blocks.reshape(slots, 2, orbitals, orbitals))


def local(features, w_first, w_second, panel, energies, pair_dest, pair_row, pair_col):
    n_dev = lax.axis_size("blk")
    my_index = lax.axis_index("blk")
    pair_count, feat_width = features.shape
    blk_dev, orbitals, columns = panel.shape
    capacity = 3 * pair_count // (2 * n_dev)
    slots = n_dev * capacity
    total_blocks = blk_dev * n_dev
    dest = pair_dest[:, 0]
    dest_table = (dest[:, None] == jnp.arange(n_dev, dtype=jnp.int32)[None, :]).astype(jnp.int32)
    rank_in = jnp.sum(jnp.cumsum(dest_table, axis=0) * dest_table, axis=1) - 1
    slot_of = dest * capacity + rank_in
    source = (
        jnp.full((slots,), pair_count, jnp.int32)
        .at[slot_of]
        .set(jnp.arange(pair_count, dtype=jnp.int32))
    )
    empty_label = jnp.full((1,), -1, jnp.int32)
    rows_sent = jnp.concatenate([pair_row, empty_label])[source]
    cols_sent = jnp.concatenate([my_index * blk_dev + pair_col, jnp.zeros((1,), jnp.int32)])[source]
    labels = jnp.stack([rows_sent, cols_sent], axis=-1).reshape(n_dev, capacity, 2)
    whole_panel = lax.all_gather(panel, "blk", axis=0, tiled=True)
    pre, hidden, blocks = predict(features, w_first, w_second, orbitals)
    padded = jnp.concatenate([blocks, jnp.zeros((1, blocks.shape[1]), jnp.bfloat16)], axis=0)
    send_blocks = padded[source].reshape(n_dev, capacity, 2, orbitals, orbitals)
    got_blocks, got_labels = (
        lax.all_to_all(send_blocks, "blk", split_axis=0, concat_axis=0, tiled=True),
        lax.all_to_all(labels, "blk", split_axis=0, concat_axis=0, tiled=True),
    )
    got_labels = got_labels.reshape(slots, 2)
    slot_panel = whole_panel[got_labels[:, 1]]
    residual, d_blocks = slot_work(
        got_blocks.reshape(slots, 2, orbitals, orbitals),
        slot_panel,
        got_labels[:, 0],
        energies,
        blk_dev,
        total_blocks,
    )
    back = lax.all_to_all(
        d_blocks.reshape(n_dev, capacity, 2, orbitals, orbitals),
        "blk",
        split_axis=0,
        concat_axis=0,
        tiled=True,
    )
    d_flat = back.reshape(slots, 2 * orbitals * orbitals)[slot_of]
    term_first, term_second = weight_terms(features, pre, hidden, d_flat, w_second, orbitals)
    grad_second = lax.psum_scatter(term_second, "blk", scatter_dimension=1, tiled=True)
    grad_first, square_sum = lax.psum((term_first, jnp.sum(residual * residual)), "blk")
    loss = (square_sum / (total_blocks * orbitals * columns)).reshape(1)
    return (residual, loss, grad_first, grad_second)


def solution(mesh):
    in_specs = (
        P(("parts", "blk"), None),
        P(),
        P(),
        P(("parts", "blk"), None, None),
        P(),
        P(("parts", "blk"), None),
        P(("parts", "blk")),
        P(("parts", "blk")),
    )
    out_specs = (P(("parts", "blk"), None, None), P("parts"), P("parts", None), P("parts", "blk"))
    n_dev = mesh.shape["blk"]
    step = functools.partial(near, z_count=4) if n_dev == 16 else local
    return jax.shard_map(step, mesh=mesh, in_specs=in_specs, out_specs=out_specs, check_vma=False)
```

```python
import functools

import jax
import jax.numpy as jnp
from jax import lax
from jax.experimental import pallas as pl
from jax.experimental.pallas import tpu as pltpu
from jax.sharding import PartitionSpec as P

BF16 = jnp.bfloat16
F32 = jnp.float32
MAIN_VMEM = 50 << 20
W_STEPS = 4


def dot(a, b, dims):
    return lax.dot_general(a, b, ((dims[:1], dims[1:]), ((), ())), preferred_element_type=F32)


def pack_kernel(dest_ref, row_ref, col_ref, feats_ref, out_ref, *, rs, blk_dev):
    pairs, f_width = feats_ref.shape
    dest = dest_ref[...]
    gid = ((dest % 2) * (2 * rs) + col_ref[...] * rs + (dest // 2) * blk_dev + row_ref[...]).astype(F32)
    out_ref[:pairs, :] = feats_ref[...]
    at = lax.broadcasted_iota(jnp.int32, (8, f_width), 0)
    label = jnp.zeros((8, f_width), F32)
    for k in range(pairs // f_width):
        label = jnp.where(at == k, gid[:, k * f_width : (k + 1) * f_width], label)
    out_ref[pairs:, :] = label.astype(BF16)


def unpack(pack_ref, k, pairs):
    at = k * (pairs + 8)
    f_width = pack_ref.shape[1]
    label = pack_ref[at + pairs : at + pairs + 8, :].astype(F32)
    label = jnp.concatenate([label[q : q + 1, :] for q in range(pairs // f_width)], axis=1)
    return pack_ref[at : at + pairs, :], label


def group_kernel(me_ref, *refs, rs, pairs, orbitals):
    *pack_refs, w_first_ref, mine_ref, theirs_ref = refs
    core = me_ref[0] % 2
    rows = lax.broadcasted_iota(jnp.int32, (4 * rs, pairs), 0)
    rows = ((rows + core * (2 * rs)) % (4 * rs)).astype(F32)
    to = 0
    for pack_ref in pack_refs:
        for k in range(pack_ref.shape[0] // (pairs + 8)):
            feats, label = unpack(pack_ref, k, pairs)
            pre = dot(feats, w_first_ref[...], (1, 0))
            hidden = (pre * (0.5 * jnp.tanh(0.5 * pre) + 0.5)).astype(BF16)
            pick = (rows == label).astype(F32).astype(BF16)
            sums = (dot(pick, hidden, (1, 0)) * (1.0 / orbitals)).astype(BF16)
            mine_ref[to : to + 2 * rs, :] = sums[: 2 * rs, :]
            theirs_ref[to : to + 2 * rs, :] = sums[2 * rs :, :]
            to += 2 * rs


def source_chip(m, chip, chips, z_count):
    x_count = chips // z_count
    return ((chip // x_count - m // x_count) % z_count) * x_count + (chip % x_count - m % x_count) % x_count


def main_kernel(*refs, chips, z_count, rows_split, half_cols, orbitals):
    me_ref, h_refs, p_refs, w_hbm = refs[0], refs[1:3], refs[3:7], refs[7]
    energies_ref, res_ref, keep_ref, send_ref, dh_ref, square_ref = refs[8:14]
    w_ref, w_sems, h_ref, c_ref, x_ref, r_ref, g_ref, l_ref = refs[14:]
    w_steps = w_sems.shape[0]
    step_cols = w_ref.shape[2] // w_steps
    w_copies = []
    for i in range(w_steps):
        cols = slice(i * step_cols, (i + 1) * step_cols)
        w_copies.append(pltpu.make_async_copy(w_hbm.at[:, cols], w_ref.at[0, :, cols], w_sems.at[i]))
        w_copies[i].start()
    me = me_ref[0]
    core = me % 2
    chip = me // 2
    listers = 2 * chips
    rs = rows_split
    half = w_ref.shape[2] // 2
    columns = energies_ref.shape[1]
    ah_count = half // 128
    total_blocks = 2 * rs
    lane = lax.broadcasted_iota(jnp.int32, (rs, 128), 1)
    low = lane < 64

    def place(lister, block):
        at = pl.multiple_of(lister * 128, 128)
        c_ref[0, pl.ds(at, 128), :] = block
        c_ref[1, pl.ds(at, 64), :] = block[64:, :]
        c_ref[1, pl.ds(at + 64, 64), :] = block[:64, :]

    x_count = chips // z_count
    for m in range(chips):
        src = source_chip(m, chip, chips, z_count)
        dz, dx = m // x_count, m % x_count
        for which, lister in ((0, 2 * src + core), (1, 2 * src + 1 - core)):
            place(lister, p_refs[2 * which + dx][dz * 128 : (dz + 1) * 128, :])
            at = pl.multiple_of(lister * rs, rs)
            for pc in range(2):
                lo = (dx * z_count + dz) * 2 * rs + pc * rs
                h_ref[pc, pl.ds(at, rs), :] = h_refs[which][lo : lo + rs, :]

    for i in range(w_steps):
        w_copies[i].wait()
        for k in range(i * step_cols // 128, (i + 1) * step_cols // 128):
            cols = slice(k * 128, (k + 1) * 128)
            w_ref[1, :, cols] = pltpu.roll(w_ref[0, :, cols].astype(F32), 64, 1).astype(BF16)

    h0, h1 = h_ref[0], h_ref[1]
    steps = half // step_cols
    per = step_cols // 128

    def forward(i, carry):
        hs, nb = i // steps, i % steps
        at = pl.multiple_of(i * step_cols, step_cols)
        y0 = dot(h0, w_ref[0, :, pl.ds(at, step_cols)], (1, 0))
        y1 = dot(h1, w_ref[1, :, pl.ds(at, step_cols)], (1, 0))
        for k in range(per):
            row = pl.multiple_of((hs * ah_count + nb * per + k) * rs, rs)
            for j in range(listers):
                v0 = y0[j * rs : (j + 1) * rs, k * 128 : (k + 1) * 128]
                v1 = y1[j * rs : (j + 1) * rs, k * 128 : (k + 1) * 128]
                cols = slice(j * 128, (j + 1) * 128)
                x_ref[0, pl.ds(row, rs), cols] = jnp.where(low, v0, v1).astype(BF16)
                x_ref[1, pl.ds(row, rs), cols] = jnp.where(low, v1, v0).astype(BF16)
        return carry

    lax.fori_loop(0, 2 * steps, forward, 0)

    energies = energies_ref[...]
    n_rows = ah_count * rs
    mb = 512
    square_ref[...] = jnp.zeros_like(square_ref)

    def product(i, carry):
        par, b = i // (n_rows // mb), i % (n_rows // mb)
        at = pl.multiple_of(b * mb, mb)
        r_h = dot(x_ref[par, pl.ds(at, mb), :], c_ref[par], (1, 0))
        r_s = dot(x_ref[par, pl.ds(n_rows + at, mb), :], c_ref[par], (1, 0))
        res = r_h - r_s * energies
        r_ref[par, pl.ds(at, mb), :] = res
        g_ref[0, par, pl.ds(at, mb), :] = (res / total_blocks).astype(BF16)
        g_ref[1, par, pl.ds(at, mb), :] = (-(res * energies) / total_blocks).astype(BF16)
        square_ref[...] += jnp.sum((res * res).reshape(mb // 8, 8, columns), axis=0)
        return carry

    lax.fori_loop(0, 2 * (n_rows // mb), product, 0)

    blk_dev = res_ref.shape[0]
    for i in range(blk_dev):
        for par in range(2):
            for ah in range(ah_count):
                res_ref[i, 2 * ah + par : 2 * ah + par + 1, :] = r_ref[
                    par, pl.ds(ah * rs + chip * blk_dev + i, 1), :
                ]

    jb_count = 8
    jb_width = jb_count * 128

    def backward(i, carry):
        hs, jb = i // (listers // jb_count), i % (listers // jb_count)
        at = pl.multiple_of(jb * jb_width, jb_width)
        d_e = dot(g_ref[hs, 0], c_ref[0, pl.ds(at, jb_width), :], (1, 1))
        d_o = dot(g_ref[hs, 1], c_ref[1, pl.ds(at, jb_width), :], (1, 1))
        for j in range(jb_count):
            row = pl.multiple_of((jb * jb_count + j) * rs, rs)
            for ah in range(ah_count):
                v0 = d_e[ah * rs : (ah + 1) * rs, j * 128 : (j + 1) * 128]
                v1 = d_o[ah * rs : (ah + 1) * rs, j * 128 : (j + 1) * 128]
                cols = pl.ds(pl.multiple_of(hs * half + ah * 128, 128), 128)
                l_ref[0, pl.ds(row, rs), cols] = jnp.where(low, v0, v1).astype(BF16)
                l_ref[1, pl.ds(row, rs), cols] = jnp.where(low, v1, v0).astype(BF16)
        return carry

    lax.fori_loop(0, 2 * (listers // jb_count), backward, 0)

    for pc in range(2):
        dh_ref[pc] = dot(l_ref[pc], w_ref[pc], (1, 1)) / orbitals

    width = 2 * half_cols
    at = pl.multiple_of(chip * width, width)
    g0 = dot(h0, l_ref[0, :, pl.ds(at, width)], (0, 0))
    g1 = dot(h1, l_ref[1, :, pl.ds(at, width)], (0, 0))
    even = core == 0
    for k in range(half_cols // 128):
        a, b = slice(k * 128, (k + 1) * 128), slice(half_cols + k * 128, half_cols + (k + 1) * 128)
        va = g0[:, a] + pltpu.roll(g1[:, a], 64, 1)
        vb = g0[:, b] + pltpu.roll(g1[:, b], 64, 1)
        keep_ref[:, a] = jnp.where(even, va, vb)
        send_ref[:, a] = jnp.where(even, vb, va)


def first_kernel(*refs, chips, z_count, rs, pairs):
    me_ref, pack_refs = refs[0], refs[1:5]
    w_first_ref, dh_ref, square_ref, first_ref, f_ref, d_ref = refs[5:]
    me = me_ref[0]
    core, chip = me % 2, me // 2
    f_width = w_first_ref.shape[0]
    x_count = chips // z_count
    group_row = (lax.broadcasted_iota(jnp.int32, (2 * rs, pairs), 0) + core * (2 * rs)).astype(F32)
    for m in range(chips):
        src = source_chip(m, chip, chips, z_count)
        dz, dx = m // x_count, m % x_count
        for which, lister in ((0, 2 * src + core), (1, 2 * src + 1 - core)):
            feats, label = unpack(pack_refs[2 * which + dx], dz, pairs)
            pre = dot(feats, w_first_ref[...], (1, 0))
            sig = 0.5 * jnp.tanh(0.5 * pre) + 0.5
            at = pl.multiple_of(lister * rs, rs)
            d_group = jnp.concatenate([dh_ref[0, pl.ds(at, rs), :], dh_ref[1, pl.ds(at, rs), :]], axis=0)
            head = d_group.astype(BF16)
            tail = (d_group - head.astype(F32)).astype(BF16)
            both = jnp.concatenate([head, tail], axis=0)
            pick = (group_row == label).astype(F32).astype(BF16)
            d_hidden = dot(jnp.concatenate([pick, pick], axis=0), both, (0, 0))
            to = pl.multiple_of(lister * pairs, pairs)
            d_ref[pl.ds(to, pairs), :] = (d_hidden * sig * (1.0 + pre * (1.0 - sig))).astype(BF16)
            f_ref[pl.ds(to, pairs), :] = feats
    first_ref[:f_width, :] = dot(f_ref[...], d_ref[...], (0, 0))
    first_ref[f_width:, :] = square_ref[...]


def combine_kernel(keep_ref, sent_ref, first_ref, got_ref, second_ref, grad_ref, loss_ref, *, count):
    second_ref[...] = keep_ref[...] + sent_ref[...]
    f_width = grad_ref.shape[0]
    grad_ref[...] = first_ref[:f_width, :] + got_ref[:f_width, :]
    square = first_ref[f_width:, :] + got_ref[f_width:, :]
    loss_ref[...] = jnp.sum(jnp.sum(square, axis=0, keepdims=True), axis=1, keepdims=True) / count


def near(features, w_first, w_second, panel, energies, pair_dest, pair_row, pair_col, z_count):
    n_dev = lax.axis_size("blk")
    me = lax.axis_index("blk").reshape(1).astype(jnp.int32)
    pairs, f_width = features.shape
    blk_dev, orbitals, columns = panel.shape
    hid, flat = w_second.shape
    chips, rs = n_dev // 2, n_dev * blk_dev // 2
    half_cols = flat // n_dev
    smem, vmem = pl.BlockSpec(memory_space=pltpu.SMEM), pl.BlockSpec(memory_space=pltpu.VMEM)
    anywhere = pl.BlockSpec(memory_space=pl.ANY)
    x_count = chips // z_count

    def to_core(v):
        return lax.ppermute(v, "blk", [(i, i ^ 1) for i in range(n_dev)])

    def from_chip(v, m):
        sends = [(2 * source_chip(m, q, chips, z_count) + c, 2 * q + c) for q in range(chips) for c in range(2)]
        return lax.ppermute(v, "blk", sends) if m else v

    def along_z(v):
        return jnp.concatenate([from_chip(v, dz * x_count) for dz in range(z_count)], axis=0)

    pack = pl.pallas_call(
        functools.partial(pack_kernel, rs=rs, blk_dev=blk_dev),
        out_shape=jax.ShapeDtypeStruct((pairs + 8, f_width), BF16),
        cost_estimate=pl.CostEstimate(flops=0, transcendentals=0, bytes_accessed=1 << 20),
        name="pack",
    )(pair_dest.reshape(1, pairs), pair_row.reshape(1, pairs), pair_col.reshape(1, pairs), features)
    packs_z = along_z(pack)
    packs = [packs_z, from_chip(packs_z, 1)]
    panels_z = along_z(panel.reshape(blk_dev * orbitals, columns))
    panels = [panels_z, from_chip(panels_z, 1)]
    h_mine, h_theirs = pl.pallas_call(
        functools.partial(group_kernel, rs=rs, pairs=pairs, orbitals=orbitals),
        out_shape=(jax.ShapeDtypeStruct((2 * rs * chips, hid), BF16),) * 2,
        in_specs=[smem] + [vmem] * 3,
        compiler_params=pltpu.CompilerParams(vmem_limit_bytes=12 << 20),
        cost_estimate=pl.CostEstimate(flops=1 << 30, transcendentals=0, bytes_accessed=1 << 21),
        name="group",
    )(me, *packs, w_first)
    h_other = to_core(h_theirs)
    panels += [to_core(v) for v in panels]
    packs += [to_core(v) for v in packs]

    listers = n_dev
    k_width = listers * 128
    n_rows = rs * orbitals // 2
    res, keep, send, d_hidden, square = pl.pallas_call(
        functools.partial(
            main_kernel, chips=chips, z_count=z_count, rows_split=rs, half_cols=half_cols, orbitals=orbitals
        ),
        out_shape=(
            jax.ShapeDtypeStruct((blk_dev, orbitals, columns), F32),
            jax.ShapeDtypeStruct((hid, half_cols), F32),
            jax.ShapeDtypeStruct((hid, half_cols), F32),
            jax.ShapeDtypeStruct((2, listers * rs, hid), F32),
            jax.ShapeDtypeStruct((8, columns), F32),
        ),
        in_specs=[smem] + [vmem] * 6 + [anywhere, vmem],
        scratch_shapes=[
            pltpu.VMEM((2, hid, flat), BF16),
            pltpu.SemaphoreType.DMA((W_STEPS,)),
            pltpu.VMEM((2, listers * rs, hid), BF16),
            pltpu.VMEM((2, k_width, columns), BF16),
            pltpu.VMEM((2, 2 * n_rows, k_width), BF16),
            pltpu.VMEM((2, n_rows, columns), F32),
            pltpu.VMEM((2, 2, n_rows, columns), BF16),
            pltpu.VMEM((2, listers * rs, flat), BF16),
        ],
        compiler_params=pltpu.CompilerParams(vmem_limit_bytes=MAIN_VMEM),
        cost_estimate=pl.CostEstimate(flops=16 * listers * rs * hid * flat, transcendentals=0, bytes_accessed=1 << 24),
        name="step",
    )(me, h_mine, h_other, *panels, w_second, energies.reshape(1, columns))
    send = to_core(send)
    first = pl.pallas_call(
        functools.partial(first_kernel, chips=chips, z_count=z_count, rs=rs, pairs=pairs),
        out_shape=jax.ShapeDtypeStruct((f_width + 8, hid), F32),
        in_specs=[smem] + [vmem] * 7,
        scratch_shapes=[pltpu.VMEM((n_dev * pairs, f_width), BF16), pltpu.VMEM((n_dev * pairs, hid), BF16)],
        compiler_params=pltpu.CompilerParams(vmem_limit_bytes=12 << 20),
        cost_estimate=pl.CostEstimate(flops=1 << 31, transcendentals=0, bytes_accessed=1 << 22),
        name="first",
    )(me, *packs, w_first, d_hidden, square)
    count = n_dev * blk_dev * orbitals * columns
    grad_second, grad_first, loss = pl.pallas_call(
        functools.partial(combine_kernel, count=count),
        out_shape=(
            jax.ShapeDtypeStruct((hid, half_cols), F32),
            jax.ShapeDtypeStruct((f_width, hid), F32),
            jax.ShapeDtypeStruct((1, 1), F32),
        ),
        compiler_params=pltpu.CompilerParams(vmem_limit_bytes=12 << 20),
        name="combine",
    )(keep, send, first, to_core(first))
    return (res, loss.reshape(1), grad_first, grad_second)


def predict(feats, w_first, w_second, orbitals):
    pre = jnp.dot(feats, w_first, preferred_element_type=jnp.float32)
    hidden = jax.nn.silu(pre).astype(jnp.bfloat16)
    blocks = (jnp.dot(hidden, w_second, preferred_element_type=jnp.float32) / orbitals).astype(
        jnp.bfloat16
    )
    return (pre, hidden, blocks)


def weight_terms(feats, pre, hidden, d_flat, w_second, orbitals):
    term_second = jnp.dot(hidden.T, d_flat, preferred_element_type=jnp.float32) / orbitals
    d_hidden = (
        lax.dot_general(
            d_flat, w_second, (((1,), (1,)), ((), ())), preferred_element_type=jnp.float32
        )
        / orbitals
    )
    sig = jax.nn.sigmoid(pre)
    d_pre = (d_hidden * sig * (1.0 + pre * (1.0 - sig))).astype(jnp.bfloat16)
    term_first = jnp.dot(feats.T, d_pre, preferred_element_type=jnp.float32)
    return (term_first, term_second)


def slot_work(slot_blocks, slot_panel, slot_rows, energies, blk_dev, total_blocks):
    slots, unused_two, orbitals, unused_o = slot_blocks.shape
    columns = slot_panel.shape[2]
    group = 32
    steps_count = slots // group
    grouped = (
        slot_blocks.reshape(steps_count, group, 2, orbitals, orbitals),
        slot_panel.reshape(steps_count, group, orbitals, columns),
        slot_rows.reshape(steps_count, group),
    )
    row_ids = jnp.arange(blk_dev, dtype=jnp.int32)

    def forward(total, item):
        blocks, coeffs, rows = item
        h_panel = jnp.einsum(
            "sab,sbp->sap", blocks[:, 0], coeffs, preferred_element_type=jnp.float32
        )
        s_panel = jnp.einsum(
            "sab,sbp->sap", blocks[:, 1], coeffs, preferred_element_type=jnp.float32
        )
        contrib = h_panel - s_panel * energies
        selector = (rows[None, :] == row_ids[:, None]).astype(jnp.float32)
        added = jnp.einsum("rs,sap->rap", selector, contrib, precision=lax.Precision.HIGHEST)
        return (total + added, None)

    residual = lax.scan(forward, jnp.zeros((blk_dev, orbitals, columns), jnp.float32), grouped)[0]
    grad_h = (residual / total_blocks).astype(jnp.bfloat16)
    grad_s = (-(residual * energies) / total_blocks).astype(jnp.bfloat16)

    def backward(carry, item):
        blocks, coeffs, rows = item
        valid = (rows >= 0)[:, None, None]
        safe_rows = jnp.maximum(rows, 0)
        gh_rows = jnp.where(valid, grad_h[safe_rows], jnp.zeros((), jnp.bfloat16))
        gs_rows = jnp.where(valid, grad_s[safe_rows], jnp.zeros((), jnp.bfloat16))
        d_h = jnp.einsum(
            "sap,sbp->sab", gh_rows, coeffs, preferred_element_type=jnp.float32
        ).astype(jnp.bfloat16)
        d_s = jnp.einsum(
            "sap,sbp->sab", gs_rows, coeffs, preferred_element_type=jnp.float32
        ).astype(jnp.bfloat16)
        return (carry, jnp.stack([d_h, d_s], axis=1))

    d_blocks = lax.scan(backward, 0, grouped)[1]
    return (residual, d_blocks.reshape(slots, 2, orbitals, orbitals))


def local(features, w_first, w_second, panel, energies, pair_dest, pair_row, pair_col):
    n_dev = lax.axis_size("blk")
    my_index = lax.axis_index("blk")
    pair_count, feat_width = features.shape
    blk_dev, orbitals, columns = panel.shape
    capacity = 3 * pair_count // (2 * n_dev)
    slots = n_dev * capacity
    total_blocks = blk_dev * n_dev
    dest = pair_dest[:, 0]
    dest_table = (dest[:, None] == jnp.arange(n_dev, dtype=jnp.int32)[None, :]).astype(jnp.int32)
    rank_in = jnp.sum(jnp.cumsum(dest_table, axis=0) * dest_table, axis=1) - 1
    slot_of = dest * capacity + rank_in
    source = (
        jnp.full((slots,), pair_count, jnp.int32)
        .at[slot_of]
        .set(jnp.arange(pair_count, dtype=jnp.int32))
    )
    empty_label = jnp.full((1,), -1, jnp.int32)
    rows_sent = jnp.concatenate([pair_row, empty_label])[source]
    cols_sent = jnp.concatenate([my_index * blk_dev + pair_col, jnp.zeros((1,), jnp.int32)])[source]
    labels = jnp.stack([rows_sent, cols_sent], axis=-1).reshape(n_dev, capacity, 2)
    whole_panel = lax.all_gather(panel, "blk", axis=0, tiled=True)
    pre, hidden, blocks = predict(features, w_first, w_second, orbitals)
    padded = jnp.concatenate([blocks, jnp.zeros((1, blocks.shape[1]), jnp.bfloat16)], axis=0)
    send_blocks = padded[source].reshape(n_dev, capacity, 2, orbitals, orbitals)
    got_blocks, got_labels = (
        lax.all_to_all(send_blocks, "blk", split_axis=0, concat_axis=0, tiled=True),
        lax.all_to_all(labels, "blk", split_axis=0, concat_axis=0, tiled=True),
    )
    got_labels = got_labels.reshape(slots, 2)
    slot_panel = whole_panel[got_labels[:, 1]]
    residual, d_blocks = slot_work(
        got_blocks.reshape(slots, 2, orbitals, orbitals),
        slot_panel,
        got_labels[:, 0],
        energies,
        blk_dev,
        total_blocks,
    )
    back = lax.all_to_all(
        d_blocks.reshape(n_dev, capacity, 2, orbitals, orbitals),
        "blk",
        split_axis=0,
        concat_axis=0,
        tiled=True,
    )
    d_flat = back.reshape(slots, 2 * orbitals * orbitals)[slot_of]
    term_first, term_second = weight_terms(features, pre, hidden, d_flat, w_second, orbitals)
    grad_second = lax.psum_scatter(term_second, "blk", scatter_dimension=1, tiled=True)
    grad_first, square_sum = lax.psum((term_first, jnp.sum(residual * residual)), "blk")
    loss = (square_sum / (total_blocks * orbitals * columns)).reshape(1)
    return (residual, loss, grad_first, grad_second)


def solution(mesh):
    in_specs = (
        P(("parts", "blk"), None),
        P(),
        P(),
        P(("parts", "blk"), None, None),
        P(),
        P(("parts", "blk"), None),
        P(("parts", "blk")),
        P(("parts", "blk")),
    )
    out_specs = (P(("parts", "blk"), None, None), P("parts"), P("parts", None), P("parts", "blk"))
    n_dev = mesh.shape["blk"]
    step = functools.partial(near, z_count=4) if n_dev == 16 else local
    return jax.shard_map(step, mesh=mesh, in_specs=in_specs, out_specs=out_specs, check_vma=False)
```

```python
import functools

import jax
import jax.numpy as jnp
from jax import lax
from jax.experimental import pallas as pl
from jax.experimental.pallas import tpu as pltpu
from jax.sharding import PartitionSpec as P

BF16 = jnp.bfloat16
F32 = jnp.float32
MAIN_VMEM = 50 << 20
W_STEPS = 4
LATE = 9


def dot(a, b, dims):
    return lax.dot_general(a, b, ((dims[:1], dims[1:]), ((), ())), preferred_element_type=F32)


def pack_kernel(dest_ref, row_ref, col_ref, feats_ref, out_ref, *, rs, blk_dev):
    pairs, f_width = feats_ref.shape
    dest = dest_ref[...]
    gid = ((dest % 2) * (2 * rs) + col_ref[...] * rs + (dest // 2) * blk_dev + row_ref[...]).astype(F32)
    out_ref[:pairs, :] = feats_ref[...]
    at = lax.broadcasted_iota(jnp.int32, (8, f_width), 0)
    label = jnp.zeros((8, f_width), F32)
    for k in range(pairs // f_width):
        label = jnp.where(at == k, gid[:, k * f_width : (k + 1) * f_width], label)
    out_ref[pairs:, :] = label.astype(BF16)


def unpack(pack_ref, k, pairs):
    at = k * (pairs + 8)
    f_width = pack_ref.shape[1]
    label = pack_ref[at + pairs : at + pairs + 8, :].astype(F32)
    label = jnp.concatenate([label[q : q + 1, :] for q in range(pairs // f_width)], axis=1)
    return pack_ref[at : at + pairs, :], label


def group_kernel(me_ref, *refs, rs, pairs, orbitals):
    *pack_refs, w_first_ref, mine_ref, theirs_ref, stack_ref = refs
    core = me_ref[0] % 2
    rows = lax.broadcasted_iota(jnp.int32, (4 * rs, pairs), 0)
    rows = ((rows + core * (2 * rs)) % (4 * rs)).astype(F32)
    for k, pack_ref in enumerate(pack_refs):
        feats, label = unpack(pack_ref, 0, pairs)
        pre = dot(feats, w_first_ref[...], (1, 0))
        hidden = (pre * (0.5 * jnp.tanh(0.5 * pre) + 0.5)).astype(BF16)
        pick = (rows == label).astype(F32).astype(BF16)
        sums = (dot(pick, hidden, (1, 0)) * (1.0 / orbitals)).astype(BF16)
        mine_ref[k * 2 * rs : (k + 1) * 2 * rs, :] = sums[: 2 * rs, :]
        theirs_ref[k * 2 * rs : (k + 1) * 2 * rs, :] = sums[2 * rs :, :]
        stack_ref[k * (pairs + 8) : (k + 1) * (pairs + 8), :] = pack_ref[...]


def source_chip(m, chip, chips, z_count):
    x_count = chips // z_count
    return ((chip // x_count - m // x_count) % z_count) * x_count + (chip % x_count - m % x_count) % x_count


def main_kernel(*refs, chips, z_count, rows_split, half_cols, orbitals):
    me_ref, h_refs, p_refs, w_hbm = refs[0], refs[1:5], refs[5:9], refs[9]
    energies_ref, res_ref, keep_ref, send_ref, dh_ref, square_ref = refs[10:16]
    w_ref, w_sems, h_ref, c_ref, x_ref, r_ref, g_ref, l_ref = refs[16:]
    w_steps = w_sems.shape[0]
    step_cols = w_ref.shape[2] // w_steps
    w_copies = []
    for i in range(w_steps):
        cols = slice(i * step_cols, (i + 1) * step_cols)
        w_copies.append(pltpu.make_async_copy(w_hbm.at[:, cols], w_ref.at[0, :, cols], w_sems.at[i]))
        w_copies[i].start()
    me = me_ref[0]
    core = me % 2
    chip = me // 2
    listers = 2 * chips
    rs = rows_split
    half = w_ref.shape[2] // 2
    columns = energies_ref.shape[1]
    ah_count = half // 128
    total_blocks = 2 * rs
    lane = lax.broadcasted_iota(jnp.int32, (rs, 128), 1)
    low = lane < 64

    def place(lister, block):
        at = pl.multiple_of(lister * 128, 128)
        c_ref[0, pl.ds(at, 128), :] = block
        c_ref[1, pl.ds(at, 64), :] = block[64:, :]
        c_ref[1, pl.ds(at + 64, 64), :] = block[:64, :]

    x_count = chips // z_count
    for m in range(chips):
        src = source_chip(m, chip, chips, z_count)
        dz, dx = m // x_count, m % x_count
        for which, lister in ((0, 2 * src + core), (1, 2 * src + 1 - core)):
            place(lister, p_refs[2 * which + dx][dz * 128 : (dz + 1) * 128, :])
            at = pl.multiple_of(lister * rs, rs)
            for pc in range(2):
                lo = dz * 2 * rs + pc * rs
                h_ref[pc, pl.ds(at, rs), :] = h_refs[2 * which + dx][lo : lo + rs, :]

    h0, h1 = h_ref[0], h_ref[1]
    per = step_cols // 128

    for i in range(w_steps):
        at = i * step_cols
        w_copies[i].wait()
        for k in range(per):
            cols = slice(at + k * 128, at + (k + 1) * 128)
            w_ref[1, :, cols] = pltpu.roll(w_ref[0, :, cols].astype(F32), 64, 1).astype(BF16)
        y0 = dot(h0, w_ref[0, :, at : at + step_cols], (1, 0))
        y1 = dot(h1, w_ref[1, :, at : at + step_cols], (1, 0))
        for k in range(per):
            row = (i * per + k) * rs
            for j in range(listers):
                v0 = y0[j * rs : (j + 1) * rs, k * 128 : (k + 1) * 128]
                v1 = y1[j * rs : (j + 1) * rs, k * 128 : (k + 1) * 128]
                cols = slice(j * 128, (j + 1) * 128)
                x_ref[0, row : row + rs, cols] = jnp.where(low, v0, v1).astype(BF16)
                x_ref[1, row : row + rs, cols] = jnp.where(low, v1, v0).astype(BF16)

    energies = energies_ref[...]
    n_rows = ah_count * rs
    mb = 512
    square_ref[...] = jnp.zeros_like(square_ref)

    def product(i, carry):
        par, b = i // (n_rows // mb), i % (n_rows // mb)
        at = pl.multiple_of(b * mb, mb)
        r_h = dot(x_ref[par, pl.ds(at, mb), :], c_ref[par], (1, 0))
        r_s = dot(x_ref[par, pl.ds(n_rows + at, mb), :], c_ref[par], (1, 0))
        res = r_h - r_s * energies
        r_ref[par, pl.ds(at, mb), :] = res
        g_ref[0, par, pl.ds(at, mb), :] = (res / total_blocks).astype(BF16)
        g_ref[1, par, pl.ds(at, mb), :] = (-(res * energies) / total_blocks).astype(BF16)
        square_ref[...] += jnp.sum((res * res).reshape(mb // 8, 8, columns), axis=0)
        return carry

    lax.fori_loop(0, 2 * (n_rows // mb), product, 0)

    blk_dev = res_ref.shape[0]
    for i in range(blk_dev):
        for par in range(2):
            for ah in range(ah_count):
                res_ref[i, 2 * ah + par : 2 * ah + par + 1, :] = r_ref[
                    par, pl.ds(ah * rs + chip * blk_dev + i, 1), :
                ]

    jb_count = 8
    jb_width = jb_count * 128

    def backward(i, carry):
        hs, jb = i // (listers // jb_count), i % (listers // jb_count)
        at = pl.multiple_of(jb * jb_width, jb_width)
        d_e = dot(g_ref[hs, 0], c_ref[0, pl.ds(at, jb_width), :], (1, 1))
        d_o = dot(g_ref[hs, 1], c_ref[1, pl.ds(at, jb_width), :], (1, 1))
        for j in range(jb_count):
            row = pl.multiple_of((jb * jb_count + j) * rs, rs)
            for ah in range(ah_count):
                v0 = d_e[ah * rs : (ah + 1) * rs, j * 128 : (j + 1) * 128]
                v1 = d_o[ah * rs : (ah + 1) * rs, j * 128 : (j + 1) * 128]
                cols = pl.ds(pl.multiple_of(hs * half + ah * 128, 128), 128)
                l_ref[0, pl.ds(row, rs), cols] = jnp.where(low, v0, v1).astype(BF16)
                l_ref[1, pl.ds(row, rs), cols] = jnp.where(low, v1, v0).astype(BF16)
        return carry

    lax.fori_loop(0, 2 * (listers // jb_count), backward, 0)

    for pc in range(2):
        dh_ref[pc] = dot(l_ref[pc], w_ref[pc], (1, 1)) / orbitals

    width = 2 * half_cols
    at = pl.multiple_of(chip * width, width)
    g0 = dot(h0, l_ref[0, :, pl.ds(at, width)], (0, 0))
    g1 = dot(h1, l_ref[1, :, pl.ds(at, width)], (0, 0))
    even = core == 0
    for k in range(half_cols // 128):
        a, b = slice(k * 128, (k + 1) * 128), slice(half_cols + k * 128, half_cols + (k + 1) * 128)
        va = g0[:, a] + pltpu.roll(g1[:, a], 64, 1)
        vb = g0[:, b] + pltpu.roll(g1[:, b], 64, 1)
        keep_ref[:, a] = jnp.where(even, va, vb)
        send_ref[:, a] = jnp.where(even, vb, va)


def first_kernel(*refs, chips, z_count, rs, pairs):
    me_ref, pack_refs = refs[0], refs[1:5]
    w_first_ref, dh_ref, square_ref, first_ref, f_ref, d_ref = refs[5:]
    me = me_ref[0]
    core, chip = me % 2, me // 2
    f_width = w_first_ref.shape[0]
    x_count = chips // z_count
    group_row = (lax.broadcasted_iota(jnp.int32, (2 * rs, pairs), 0) + core * (2 * rs)).astype(F32)
    for m in range(chips):
        src = source_chip(m, chip, chips, z_count)
        dz, dx = m // x_count, m % x_count
        for which, lister in ((0, 2 * src + core), (1, 2 * src + 1 - core)):
            feats, label = unpack(pack_refs[2 * which + dx], dz, pairs)
            pre = dot(feats, w_first_ref[...], (1, 0))
            sig = 0.5 * jnp.tanh(0.5 * pre) + 0.5
            at = pl.multiple_of(lister * rs, rs)
            d_group = jnp.concatenate([dh_ref[0, pl.ds(at, rs), :], dh_ref[1, pl.ds(at, rs), :]], axis=0)
            head = d_group.astype(BF16)
            tail = (d_group - head.astype(F32)).astype(BF16)
            both = jnp.concatenate([head, tail], axis=0)
            pick = (group_row == label).astype(F32).astype(BF16)
            d_hidden = dot(jnp.concatenate([pick, pick], axis=0), both, (0, 0))
            to = pl.multiple_of(lister * pairs, pairs)
            d_ref[pl.ds(to, pairs), :] = (d_hidden * sig * (1.0 + pre * (1.0 - sig))).astype(BF16)
            f_ref[pl.ds(to, pairs), :] = feats
    first_ref[:f_width, :] = dot(f_ref[...], d_ref[...], (0, 0))
    first_ref[f_width:, :] = square_ref[...]


def combine_kernel(keep_ref, sent_ref, first_ref, got_ref, second_ref, grad_ref, loss_ref, *, count):
    second_ref[...] = keep_ref[...] + sent_ref[...]
    f_width = grad_ref.shape[0]
    grad_ref[...] = first_ref[:f_width, :] + got_ref[:f_width, :]
    square = first_ref[f_width:, :] + got_ref[f_width:, :]
    loss_ref[...] = jnp.sum(jnp.sum(square, axis=0, keepdims=True), axis=1, keepdims=True) / count


def near(features, w_first, w_second, panel, energies, pair_dest, pair_row, pair_col, z_count):
    n_dev = lax.axis_size("blk")
    me = lax.axis_index("blk").reshape(1).astype(jnp.int32)
    pairs, f_width = features.shape
    blk_dev, orbitals, columns = panel.shape
    hid, flat = w_second.shape
    chips, rs = n_dev // 2, n_dev * blk_dev // 2
    half_cols = flat // n_dev
    smem, vmem = pl.BlockSpec(memory_space=pltpu.SMEM), pl.BlockSpec(memory_space=pltpu.VMEM)
    anywhere = pl.BlockSpec(memory_space=pl.ANY)
    x_count = chips // z_count

    def to_core(v):
        return lax.ppermute(v, "blk", [(i, i ^ 1) for i in range(n_dev)])

    def from_chip(v, m):
        sends = [(2 * source_chip(m, q, chips, z_count) + c, 2 * q + c) for q in range(chips) for c in range(2)]
        return lax.ppermute(v, "blk", sends) if m else v

    pack = pl.pallas_call(
        functools.partial(pack_kernel, rs=rs, blk_dev=blk_dev),
        out_shape=jax.ShapeDtypeStruct((pairs + 8, f_width), BF16),
        cost_estimate=pl.CostEstimate(flops=0, transcendentals=0, bytes_accessed=1 << 20),
        name="pack",
    )(pair_dest.reshape(1, pairs), pair_row.reshape(1, pairs), pair_col.reshape(1, pairs), features)
    def to_both(v):
        sends = [(2 * source_chip(1, q, chips, z_count) + 1 - c, 2 * q + c) for q in range(chips) for c in range(2)]
        return lax.ppermute(v, "blk", sends)

    rows = panel.reshape(blk_dev * orbitals, columns)
    rows_late, pack = lax.optimization_barrier((rows, pack))
    packs = [from_chip(pack, dz * x_count) for dz in range(z_count)]
    panels_z = [rows] + [from_chip(rows if dz < LATE else rows_late, dz * x_count) for dz in range(1, z_count)]
    panels_z = jnp.concatenate(panels_z, axis=0)
    panels = [panels_z, from_chip(panels_z, 1)]
    h_mine, h_theirs, packs_z = pl.pallas_call(
        functools.partial(group_kernel, rs=rs, pairs=pairs, orbitals=orbitals),
        out_shape=(
            jax.ShapeDtypeStruct((2 * rs * z_count, hid), BF16),
            jax.ShapeDtypeStruct((2 * rs * z_count, hid), BF16),
            jax.ShapeDtypeStruct((z_count * (pairs + 8), f_width), BF16),
        ),
        in_specs=[smem] + [vmem] * (z_count + 1),
        compiler_params=pltpu.CompilerParams(vmem_limit_bytes=12 << 20),
        cost_estimate=pl.CostEstimate(flops=1 << 34, transcendentals=0, bytes_accessed=1 << 21),
        name="group",
    )(me, *packs, w_first)
    hiddens = [h_mine, from_chip(h_mine, 1), to_core(h_theirs), to_both(h_theirs)]
    panels[1], packs_z = lax.optimization_barrier((panels[1], packs_z))
    panels += [to_core(v) for v in panels]
    packs = [packs_z, from_chip(packs_z, 1), to_core(packs_z), to_both(packs_z)]

    listers = n_dev
    k_width = listers * 128
    n_rows = rs * orbitals // 2
    res, keep, send, d_hidden, square = pl.pallas_call(
        functools.partial(
            main_kernel, chips=chips, z_count=z_count, rows_split=rs, half_cols=half_cols, orbitals=orbitals
        ),
        out_shape=(
            jax.ShapeDtypeStruct((blk_dev, orbitals, columns), F32),
            jax.ShapeDtypeStruct((hid, half_cols), F32),
            jax.ShapeDtypeStruct((hid, half_cols), F32),
            jax.ShapeDtypeStruct((2, listers * rs, hid), F32),
            jax.ShapeDtypeStruct((8, columns), F32),
        ),
        in_specs=[smem] + [vmem] * 8 + [anywhere, vmem],
        scratch_shapes=[
            pltpu.VMEM((2, hid, flat), BF16),
            pltpu.SemaphoreType.DMA((W_STEPS,)),
            pltpu.VMEM((2, listers * rs, hid), BF16),
            pltpu.VMEM((2, k_width, columns), BF16),
            pltpu.VMEM((2, 2 * n_rows, k_width), BF16),
            pltpu.VMEM((2, n_rows, columns), F32),
            pltpu.VMEM((2, 2, n_rows, columns), BF16),
            pltpu.VMEM((2, listers * rs, flat), BF16),
        ],
        compiler_params=pltpu.CompilerParams(vmem_limit_bytes=MAIN_VMEM),
        cost_estimate=pl.CostEstimate(flops=1 << 29, transcendentals=0, bytes_accessed=1 << 20),
        name="step",
    )(me, *hiddens, *panels, w_second, energies.reshape(1, columns))
    send = to_core(send)
    first = pl.pallas_call(
        functools.partial(first_kernel, chips=chips, z_count=z_count, rs=rs, pairs=pairs),
        out_shape=jax.ShapeDtypeStruct((f_width + 8, hid), F32),
        in_specs=[smem] + [vmem] * 7,
        scratch_shapes=[pltpu.VMEM((n_dev * pairs, f_width), BF16), pltpu.VMEM((n_dev * pairs, hid), BF16)],
        compiler_params=pltpu.CompilerParams(vmem_limit_bytes=12 << 20),
        cost_estimate=pl.CostEstimate(flops=1 << 31, transcendentals=0, bytes_accessed=1 << 22),
        name="first",
    )(me, *packs, w_first, d_hidden, square)
    count = n_dev * blk_dev * orbitals * columns
    grad_second, grad_first, loss = pl.pallas_call(
        functools.partial(combine_kernel, count=count),
        out_shape=(
            jax.ShapeDtypeStruct((hid, half_cols), F32),
            jax.ShapeDtypeStruct((f_width, hid), F32),
            jax.ShapeDtypeStruct((1, 1), F32),
        ),
        compiler_params=pltpu.CompilerParams(vmem_limit_bytes=12 << 20),
        name="combine",
    )(keep, send, first, to_core(first))
    return (res, loss.reshape(1), grad_first, grad_second)


def predict(feats, w_first, w_second, orbitals):
    pre = jnp.dot(feats, w_first, preferred_element_type=jnp.float32)
    hidden = jax.nn.silu(pre).astype(jnp.bfloat16)
    blocks = (jnp.dot(hidden, w_second, preferred_element_type=jnp.float32) / orbitals).astype(
        jnp.bfloat16
    )
    return (pre, hidden, blocks)


def weight_terms(feats, pre, hidden, d_flat, w_second, orbitals):
    term_second = jnp.dot(hidden.T, d_flat, preferred_element_type=jnp.float32) / orbitals
    d_hidden = (
        lax.dot_general(
            d_flat, w_second, (((1,), (1,)), ((), ())), preferred_element_type=jnp.float32
        )
        / orbitals
    )
    sig = jax.nn.sigmoid(pre)
    d_pre = (d_hidden * sig * (1.0 + pre * (1.0 - sig))).astype(jnp.bfloat16)
    term_first = jnp.dot(feats.T, d_pre, preferred_element_type=jnp.float32)
    return (term_first, term_second)


def slot_work(slot_blocks, slot_panel, slot_rows, energies, blk_dev, total_blocks):
    slots, unused_two, orbitals, unused_o = slot_blocks.shape
    columns = slot_panel.shape[2]
    group = 32
    steps_count = slots // group
    grouped = (
        slot_blocks.reshape(steps_count, group, 2, orbitals, orbitals),
        slot_panel.reshape(steps_count, group, orbitals, columns),
        slot_rows.reshape(steps_count, group),
    )
    row_ids = jnp.arange(blk_dev, dtype=jnp.int32)

    def forward(total, item):
        blocks, coeffs, rows = item
        h_panel = jnp.einsum(
            "sab,sbp->sap", blocks[:, 0], coeffs, preferred_element_type=jnp.float32
        )
        s_panel = jnp.einsum(
            "sab,sbp->sap", blocks[:, 1], coeffs, preferred_element_type=jnp.float32
        )
        contrib = h_panel - s_panel * energies
        selector = (rows[None, :] == row_ids[:, None]).astype(jnp.float32)
        added = jnp.einsum("rs,sap->rap", selector, contrib, precision=lax.Precision.HIGHEST)
        return (total + added, None)

    residual = lax.scan(forward, jnp.zeros((blk_dev, orbitals, columns), jnp.float32), grouped)[0]
    grad_h = (residual / total_blocks).astype(jnp.bfloat16)
    grad_s = (-(residual * energies) / total_blocks).astype(jnp.bfloat16)

    def backward(carry, item):
        blocks, coeffs, rows = item
        valid = (rows >= 0)[:, None, None]
        safe_rows = jnp.maximum(rows, 0)
        gh_rows = jnp.where(valid, grad_h[safe_rows], jnp.zeros((), jnp.bfloat16))
        gs_rows = jnp.where(valid, grad_s[safe_rows], jnp.zeros((), jnp.bfloat16))
        d_h = jnp.einsum(
            "sap,sbp->sab", gh_rows, coeffs, preferred_element_type=jnp.float32
        ).astype(jnp.bfloat16)
        d_s = jnp.einsum(
            "sap,sbp->sab", gs_rows, coeffs, preferred_element_type=jnp.float32
        ).astype(jnp.bfloat16)
        return (carry, jnp.stack([d_h, d_s], axis=1))

    d_blocks = lax.scan(backward, 0, grouped)[1]
    return (residual, d_blocks.reshape(slots, 2, orbitals, orbitals))


def local(features, w_first, w_second, panel, energies, pair_dest, pair_row, pair_col):
    n_dev = lax.axis_size("blk")
    my_index = lax.axis_index("blk")
    pair_count, feat_width = features.shape
    blk_dev, orbitals, columns = panel.shape
    capacity = 3 * pair_count // (2 * n_dev)
    slots = n_dev * capacity
    total_blocks = blk_dev * n_dev
    dest = pair_dest[:, 0]
    dest_table = (dest[:, None] == jnp.arange(n_dev, dtype=jnp.int32)[None, :]).astype(jnp.int32)
    rank_in = jnp.sum(jnp.cumsum(dest_table, axis=0) * dest_table, axis=1) - 1
    slot_of = dest * capacity + rank_in
    source = (
        jnp.full((slots,), pair_count, jnp.int32)
        .at[slot_of]
        .set(jnp.arange(pair_count, dtype=jnp.int32))
    )
    empty_label = jnp.full((1,), -1, jnp.int32)
    rows_sent = jnp.concatenate([pair_row, empty_label])[source]
    cols_sent = jnp.concatenate([my_index * blk_dev + pair_col, jnp.zeros((1,), jnp.int32)])[source]
    labels = jnp.stack([rows_sent, cols_sent], axis=-1).reshape(n_dev, capacity, 2)
    whole_panel = lax.all_gather(panel, "blk", axis=0, tiled=True)
    pre, hidden, blocks = predict(features, w_first, w_second, orbitals)
    padded = jnp.concatenate([blocks, jnp.zeros((1, blocks.shape[1]), jnp.bfloat16)], axis=0)
    send_blocks = padded[source].reshape(n_dev, capacity, 2, orbitals, orbitals)
    got_blocks, got_labels = (
        lax.all_to_all(send_blocks, "blk", split_axis=0, concat_axis=0, tiled=True),
        lax.all_to_all(labels, "blk", split_axis=0, concat_axis=0, tiled=True),
    )
    got_labels = got_labels.reshape(slots, 2)
    slot_panel = whole_panel[got_labels[:, 1]]
    residual, d_blocks = slot_work(
        got_blocks.reshape(slots, 2, orbitals, orbitals),
        slot_panel,
        got_labels[:, 0],
        energies,
        blk_dev,
        total_blocks,
    )
    back = lax.all_to_all(
        d_blocks.reshape(n_dev, capacity, 2, orbitals, orbitals),
        "blk",
        split_axis=0,
        concat_axis=0,
        tiled=True,
    )
    d_flat = back.reshape(slots, 2 * orbitals * orbitals)[slot_of]
    term_first, term_second = weight_terms(features, pre, hidden, d_flat, w_second, orbitals)
    grad_second = lax.psum_scatter(term_second, "blk", scatter_dimension=1, tiled=True)
    grad_first, square_sum = lax.psum((term_first, jnp.sum(residual * residual)), "blk")
    loss = (square_sum / (total_blocks * orbitals * columns)).reshape(1)
    return (residual, loss, grad_first, grad_second)


def solution(mesh):
    in_specs = (
        P(("parts", "blk"), None),
        P(),
        P(),
        P(("parts", "blk"), None, None),
        P(),
        P(("parts", "blk"), None),
        P(("parts", "blk")),
        P(("parts", "blk")),
    )
    out_specs = (P(("parts", "blk"), None, None), P("parts"), P("parts", None), P("parts", "blk"))
    n_dev = mesh.shape["blk"]
    step = functools.partial(near, z_count=4) if n_dev == 16 else local
    return jax.shard_map(step, mesh=mesh, in_specs=in_specs, out_specs=out_specs, check_vma=False)
```

```python
import functools

import jax
import jax.numpy as jnp
from jax import lax
from jax.experimental import pallas as pl
from jax.experimental.pallas import tpu as pltpu
from jax.sharding import PartitionSpec as P

BF16 = jnp.bfloat16
F32 = jnp.float32
MAIN_VMEM = 50 << 20
W_STEPS = 4
LATE = 9


def dot(a, b, dims):
    return lax.dot_general(a, b, ((dims[:1], dims[1:]), ((), ())), preferred_element_type=F32)


def pack_kernel(dest_ref, row_ref, col_ref, feats_ref, out_ref, *, rs, blk_dev):
    pairs, f_width = feats_ref.shape
    dest = dest_ref[...]
    gid = ((dest % 2) * (2 * rs) + col_ref[...] * rs + (dest // 2) * blk_dev + row_ref[...]).astype(F32)
    out_ref[:pairs, :] = feats_ref[...]
    at = lax.broadcasted_iota(jnp.int32, (8, f_width), 0)
    label = jnp.zeros((8, f_width), F32)
    for k in range(pairs // f_width):
        label = jnp.where(at == k, gid[:, k * f_width : (k + 1) * f_width], label)
    out_ref[pairs:, :] = label.astype(BF16)


def unpack(pack_ref, k, pairs):
    at = k * (pairs + 8)
    f_width = pack_ref.shape[1]
    label = pack_ref[at + pairs : at + pairs + 8, :].astype(F32)
    label = jnp.concatenate([label[q : q + 1, :] for q in range(pairs // f_width)], axis=1)
    return pack_ref[at : at + pairs, :], label


def group_kernel(me_ref, *refs, rs, pairs, orbitals):
    *pack_refs, w_first_ref, mine_ref, theirs_ref, stack_ref = refs
    core = me_ref[0] % 2
    rows = lax.broadcasted_iota(jnp.int32, (4 * rs, pairs), 0)
    rows = ((rows + core * (2 * rs)) % (4 * rs)).astype(F32)
    for k, pack_ref in enumerate(pack_refs):
        feats, label = unpack(pack_ref, 0, pairs)
        pre = dot(feats, w_first_ref[...], (1, 0))
        hidden = (pre * (0.5 * jnp.tanh(0.5 * pre) + 0.5)).astype(BF16)
        pick = (rows == label).astype(F32).astype(BF16)
        sums = (dot(pick, hidden, (1, 0)) * (1.0 / orbitals)).astype(BF16)
        mine_ref[k * 2 * rs : (k + 1) * 2 * rs, :] = sums[: 2 * rs, :]
        theirs_ref[k * 2 * rs : (k + 1) * 2 * rs, :] = sums[2 * rs :, :]
        stack_ref[k * (pairs + 8) : (k + 1) * (pairs + 8), :] = pack_ref[...]


def source_chip(m, chip, chips, z_count):
    x_count = chips // z_count
    return ((chip // x_count - m // x_count) % z_count) * x_count + (chip % x_count - m % x_count) % x_count


def main_kernel(*refs, chips, z_count, rows_split, half_cols, orbitals):
    me_ref, h_refs, p_refs, w_hbm = refs[0], refs[1:5], refs[5:9], refs[9]
    energies_ref, res_ref, keep_ref, send_ref, dh_ref, square_ref = refs[10:16]
    w_ref, w_sems, h_ref, c_ref, x_ref, r_ref, g_ref, l_ref = refs[16:]
    w_steps = w_sems.shape[0]
    step_cols = w_ref.shape[2] // w_steps
    w_copies = []
    for i in range(w_steps):
        cols = slice(i * step_cols, (i + 1) * step_cols)
        w_copies.append(pltpu.make_async_copy(w_hbm.at[:, cols], w_ref.at[0, :, cols], w_sems.at[i]))
        w_copies[i].start()
    me = me_ref[0]
    core = me % 2
    chip = me // 2
    listers = 2 * chips
    rs = rows_split
    half = w_ref.shape[2] // 2
    columns = energies_ref.shape[1]
    ah_count = half // 128
    total_blocks = 2 * rs
    lane = lax.broadcasted_iota(jnp.int32, (rs, 128), 1)
    low = lane < 64

    def place(lister, block):
        at = pl.multiple_of(lister * 128, 128)
        c_ref[0, pl.ds(at, 128), :] = block
        c_ref[1, pl.ds(at, 64), :] = block[64:, :]
        c_ref[1, pl.ds(at + 64, 64), :] = block[:64, :]

    x_count = chips // z_count
    for m in range(chips):
        src = source_chip(m, chip, chips, z_count)
        dz, dx = m // x_count, m % x_count
        for which, lister in ((0, 2 * src + core), (1, 2 * src + 1 - core)):
            place(lister, p_refs[2 * which + dx][dz * 128 : (dz + 1) * 128, :])
            at = pl.multiple_of(lister * rs, rs)
            for pc in range(2):
                lo = dz * 2 * rs + pc * rs
                h_ref[pc, pl.ds(at, rs), :] = h_refs[2 * which + dx][lo : lo + rs, :]

    h0, h1 = h_ref[0], h_ref[1]
    per = step_cols // 128

    for i in range(w_steps):
        at = i * step_cols
        w_copies[i].wait()
        for k in range(per):
            cols = slice(at + k * 128, at + (k + 1) * 128)
            w_ref[1, :, cols] = pltpu.roll(w_ref[0, :, cols].astype(F32), 64, 1).astype(BF16)
        y0 = dot(h0, w_ref[0, :, at : at + step_cols], (1, 0))
        y1 = dot(h1, w_ref[1, :, at : at + step_cols], (1, 0))
        for k in range(per):
            row = (i * per + k) * rs
            for j in range(listers):
                v0 = y0[j * rs : (j + 1) * rs, k * 128 : (k + 1) * 128]
                v1 = y1[j * rs : (j + 1) * rs, k * 128 : (k + 1) * 128]
                cols = slice(j * 128, (j + 1) * 128)
                x_ref[0, row : row + rs, cols] = jnp.where(low, v0, v1).astype(BF16)
                x_ref[1, row : row + rs, cols] = jnp.where(low, v1, v0).astype(BF16)

    energies = energies_ref[...]
    n_rows = ah_count * rs
    mb = 512
    square_ref[...] = jnp.zeros_like(square_ref)

    def product(i, carry):
        par, b = i // (n_rows // mb), i % (n_rows // mb)
        at = pl.multiple_of(b * mb, mb)
        r_h = dot(x_ref[par, pl.ds(at, mb), :], c_ref[par], (1, 0))
        r_s = dot(x_ref[par, pl.ds(n_rows + at, mb), :], c_ref[par], (1, 0))
        res = r_h - r_s * energies
        r_ref[par, pl.ds(at, mb), :] = res
        g_ref[0, par, pl.ds(at, mb), :] = (res / total_blocks).astype(BF16)
        g_ref[1, par, pl.ds(at, mb), :] = (-(res * energies) / total_blocks).astype(BF16)
        square_ref[...] += jnp.sum((res * res).reshape(mb // 8, 8, columns), axis=0)
        return carry

    lax.fori_loop(0, 2 * (n_rows // mb), product, 0)

    blk_dev = res_ref.shape[0]
    for i in range(blk_dev):
        for par in range(2):
            for ah in range(ah_count):
                res_ref[i, 2 * ah + par : 2 * ah + par + 1, :] = r_ref[
                    par, pl.ds(ah * rs + chip * blk_dev + i, 1), :
                ]

    jb_count = 8
    jb_width = jb_count * 128

    for i in range(2 * (listers // jb_count)):
        hs, jb = i // (listers // jb_count), i % (listers // jb_count)
        at = jb * jb_width
        d_e = dot(g_ref[hs, 0], c_ref[0, pl.ds(at, jb_width), :], (1, 1))
        d_o = dot(g_ref[hs, 1], c_ref[1, pl.ds(at, jb_width), :], (1, 1))
        for j in range(jb_count):
            row = (jb * jb_count + j) * rs
            for ah in range(ah_count):
                v0 = d_e[ah * rs : (ah + 1) * rs, j * 128 : (j + 1) * 128]
                v1 = d_o[ah * rs : (ah + 1) * rs, j * 128 : (j + 1) * 128]
                cols = slice(hs * half + ah * 128, hs * half + (ah + 1) * 128)
                l_ref[0, pl.ds(row, rs), cols] = jnp.where(low, v0, v1).astype(BF16)
                l_ref[1, pl.ds(row, rs), cols] = jnp.where(low, v1, v0).astype(BF16)

    for pc in range(2):
        dh_ref[pc] = dot(l_ref[pc], w_ref[pc], (1, 1)) / orbitals

    width = 2 * half_cols
    at = pl.multiple_of(chip * width, width)
    g0 = dot(h0, l_ref[0, :, pl.ds(at, width)], (0, 0))
    g1 = dot(h1, l_ref[1, :, pl.ds(at, width)], (0, 0))
    even = core == 0
    for k in range(half_cols // 128):
        a, b = slice(k * 128, (k + 1) * 128), slice(half_cols + k * 128, half_cols + (k + 1) * 128)
        va = g0[:, a] + pltpu.roll(g1[:, a], 64, 1)
        vb = g0[:, b] + pltpu.roll(g1[:, b], 64, 1)
        keep_ref[:, a] = jnp.where(even, va, vb)
        send_ref[:, a] = jnp.where(even, vb, va)


def first_kernel(*refs, chips, z_count, rs, pairs):
    me_ref, pack_refs = refs[0], refs[1:5]
    w_first_ref, dh_ref, square_ref, first_ref, f_ref, d_ref = refs[5:]
    me = me_ref[0]
    core, chip = me % 2, me // 2
    f_width = w_first_ref.shape[0]
    x_count = chips // z_count
    group_row = (lax.broadcasted_iota(jnp.int32, (2 * rs, pairs), 0) + core * (2 * rs)).astype(F32)
    for m in range(chips):
        src = source_chip(m, chip, chips, z_count)
        dz, dx = m // x_count, m % x_count
        for which, lister in ((0, 2 * src + core), (1, 2 * src + 1 - core)):
            feats, label = unpack(pack_refs[2 * which + dx], dz, pairs)
            pre = dot(feats, w_first_ref[...], (1, 0))
            sig = 0.5 * jnp.tanh(0.5 * pre) + 0.5
            at = pl.multiple_of(lister * rs, rs)
            d_group = jnp.concatenate([dh_ref[0, pl.ds(at, rs), :], dh_ref[1, pl.ds(at, rs), :]], axis=0)
            head = d_group.astype(BF16)
            tail = (d_group - head.astype(F32)).astype(BF16)
            both = jnp.concatenate([head, tail], axis=0)
            pick = (group_row == label).astype(F32).astype(BF16)
            d_hidden = dot(jnp.concatenate([pick, pick], axis=0), both, (0, 0))
            to = pl.multiple_of(lister * pairs, pairs)
            d_ref[pl.ds(to, pairs), :] = (d_hidden * sig * (1.0 + pre * (1.0 - sig))).astype(BF16)
            f_ref[pl.ds(to, pairs), :] = feats
    first_ref[:f_width, :] = dot(f_ref[...], d_ref[...], (0, 0))
    first_ref[f_width:, :] = square_ref[...]


def combine_kernel(keep_ref, sent_ref, first_ref, got_ref, second_ref, grad_ref, loss_ref, *, count):
    second_ref[...] = keep_ref[...] + sent_ref[...]
    f_width = grad_ref.shape[0]
    grad_ref[...] = first_ref[:f_width, :] + got_ref[:f_width, :]
    square = first_ref[f_width:, :] + got_ref[f_width:, :]
    loss_ref[...] = jnp.sum(jnp.sum(square, axis=0, keepdims=True), axis=1, keepdims=True) / count


def near(features, w_first, w_second, panel, energies, pair_dest, pair_row, pair_col, z_count):
    n_dev = lax.axis_size("blk")
    me = lax.axis_index("blk").reshape(1).astype(jnp.int32)
    pairs, f_width = features.shape
    blk_dev, orbitals, columns = panel.shape
    hid, flat = w_second.shape
    chips, rs = n_dev // 2, n_dev * blk_dev // 2
    half_cols = flat // n_dev
    smem, vmem = pl.BlockSpec(memory_space=pltpu.SMEM), pl.BlockSpec(memory_space=pltpu.VMEM)
    anywhere = pl.BlockSpec(memory_space=pl.ANY)
    x_count = chips // z_count

    def to_core(v):
        return lax.ppermute(v, "blk", [(i, i ^ 1) for i in range(n_dev)])

    def from_chip(v, m):
        sends = [(2 * source_chip(m, q, chips, z_count) + c, 2 * q + c) for q in range(chips) for c in range(2)]
        return lax.ppermute(v, "blk", sends) if m else v

    pack = pl.pallas_call(
        functools.partial(pack_kernel, rs=rs, blk_dev=blk_dev),
        out_shape=jax.ShapeDtypeStruct((pairs + 8, f_width), BF16),
        cost_estimate=pl.CostEstimate(flops=0, transcendentals=0, bytes_accessed=1 << 20),
        name="pack",
    )(pair_dest.reshape(1, pairs), pair_row.reshape(1, pairs), pair_col.reshape(1, pairs), features)
    def to_both(v):
        sends = [(2 * source_chip(1, q, chips, z_count) + 1 - c, 2 * q + c) for q in range(chips) for c in range(2)]
        return lax.ppermute(v, "blk", sends)

    rows = panel.reshape(blk_dev * orbitals, columns)
    rows_late, pack = lax.optimization_barrier((rows, pack))
    packs = [from_chip(pack, dz * x_count) for dz in range(z_count)]
    panels_z = [rows] + [from_chip(rows if dz < LATE else rows_late, dz * x_count) for dz in range(1, z_count)]
    panels_z = jnp.concatenate(panels_z, axis=0)
    panels = [panels_z, from_chip(panels_z, 1)]
    h_mine, h_theirs, packs_z = pl.pallas_call(
        functools.partial(group_kernel, rs=rs, pairs=pairs, orbitals=orbitals),
        out_shape=(
            jax.ShapeDtypeStruct((2 * rs * z_count, hid), BF16),
            jax.ShapeDtypeStruct((2 * rs * z_count, hid), BF16),
            jax.ShapeDtypeStruct((z_count * (pairs + 8), f_width), BF16),
        ),
        in_specs=[smem] + [vmem] * (z_count + 1),
        compiler_params=pltpu.CompilerParams(vmem_limit_bytes=12 << 20),
        cost_estimate=pl.CostEstimate(flops=1 << 34, transcendentals=0, bytes_accessed=1 << 21),
        name="group",
    )(me, *packs, w_first)
    hiddens = [h_mine, from_chip(h_mine, 1), to_core(h_theirs), to_both(h_theirs)]
    panels[1], packs_z = lax.optimization_barrier((panels[1], packs_z))
    panels += [to_core(v) for v in panels]
    packs = [packs_z, from_chip(packs_z, 1), to_core(packs_z), to_both(packs_z)]

    listers = n_dev
    k_width = listers * 128
    n_rows = rs * orbitals // 2
    res, keep, send, d_hidden, square = pl.pallas_call(
        functools.partial(
            main_kernel, chips=chips, z_count=z_count, rows_split=rs, half_cols=half_cols, orbitals=orbitals
        ),
        out_shape=(
            jax.ShapeDtypeStruct((blk_dev, orbitals, columns), F32),
            jax.ShapeDtypeStruct((hid, half_cols), F32),
            jax.ShapeDtypeStruct((hid, half_cols), F32),
            jax.ShapeDtypeStruct((2, listers * rs, hid), F32),
            jax.ShapeDtypeStruct((8, columns), F32),
        ),
        in_specs=[smem] + [vmem] * 8 + [anywhere, vmem],
        scratch_shapes=[
            pltpu.VMEM((2, hid, flat), BF16),
            pltpu.SemaphoreType.DMA((W_STEPS,)),
            pltpu.VMEM((2, listers * rs, hid), BF16),
            pltpu.VMEM((2, k_width, columns), BF16),
            pltpu.VMEM((2, 2 * n_rows, k_width), BF16),
            pltpu.VMEM((2, n_rows, columns), F32),
            pltpu.VMEM((2, 2, n_rows, columns), BF16),
            pltpu.VMEM((2, listers * rs, flat), BF16),
        ],
        compiler_params=pltpu.CompilerParams(vmem_limit_bytes=MAIN_VMEM),
        cost_estimate=pl.CostEstimate(flops=1 << 29, transcendentals=0, bytes_accessed=1 << 20),
        name="step",
    )(me, *hiddens, *panels, w_second, energies.reshape(1, columns))
    send = to_core(send)
    first = pl.pallas_call(
        functools.partial(first_kernel, chips=chips, z_count=z_count, rs=rs, pairs=pairs),
        out_shape=jax.ShapeDtypeStruct((f_width + 8, hid), F32),
        in_specs=[smem] + [vmem] * 7,
        scratch_shapes=[pltpu.VMEM((n_dev * pairs, f_width), BF16), pltpu.VMEM((n_dev * pairs, hid), BF16)],
        compiler_params=pltpu.CompilerParams(vmem_limit_bytes=12 << 20),
        cost_estimate=pl.CostEstimate(flops=1 << 31, transcendentals=0, bytes_accessed=1 << 22),
        name="first",
    )(me, *packs, w_first, d_hidden, square)
    count = n_dev * blk_dev * orbitals * columns
    grad_second, grad_first, loss = pl.pallas_call(
        functools.partial(combine_kernel, count=count),
        out_shape=(
            jax.ShapeDtypeStruct((hid, half_cols), F32),
            jax.ShapeDtypeStruct((f_width, hid), F32),
            jax.ShapeDtypeStruct((1, 1), F32),
        ),
        compiler_params=pltpu.CompilerParams(vmem_limit_bytes=12 << 20),
        name="combine",
    )(keep, send, first, to_core(first))
    return (res, loss.reshape(1), grad_first, grad_second)


def predict(feats, w_first, w_second, orbitals):
    pre = jnp.dot(feats, w_first, preferred_element_type=jnp.float32)
    hidden = jax.nn.silu(pre).astype(jnp.bfloat16)
    blocks = (jnp.dot(hidden, w_second, preferred_element_type=jnp.float32) / orbitals).astype(
        jnp.bfloat16
    )
    return (pre, hidden, blocks)


def weight_terms(feats, pre, hidden, d_flat, w_second, orbitals):
    term_second = jnp.dot(hidden.T, d_flat, preferred_element_type=jnp.float32) / orbitals
    d_hidden = (
        lax.dot_general(
            d_flat, w_second, (((1,), (1,)), ((), ())), preferred_element_type=jnp.float32
        )
        / orbitals
    )
    sig = jax.nn.sigmoid(pre)
    d_pre = (d_hidden * sig * (1.0 + pre * (1.0 - sig))).astype(jnp.bfloat16)
    term_first = jnp.dot(feats.T, d_pre, preferred_element_type=jnp.float32)
    return (term_first, term_second)


def slot_work(slot_blocks, slot_panel, slot_rows, energies, blk_dev, total_blocks):
    slots, unused_two, orbitals, unused_o = slot_blocks.shape
    columns = slot_panel.shape[2]
    group = 32
    steps_count = slots // group
    grouped = (
        slot_blocks.reshape(steps_count, group, 2, orbitals, orbitals),
        slot_panel.reshape(steps_count, group, orbitals, columns),
        slot_rows.reshape(steps_count, group),
    )
    row_ids = jnp.arange(blk_dev, dtype=jnp.int32)

    def forward(total, item):
        blocks, coeffs, rows = item
        h_panel = jnp.einsum(
            "sab,sbp->sap", blocks[:, 0], coeffs, preferred_element_type=jnp.float32
        )
        s_panel = jnp.einsum(
            "sab,sbp->sap", blocks[:, 1], coeffs, preferred_element_type=jnp.float32
        )
        contrib = h_panel - s_panel * energies
        selector = (rows[None, :] == row_ids[:, None]).astype(jnp.float32)
        added = jnp.einsum("rs,sap->rap", selector, contrib, precision=lax.Precision.HIGHEST)
        return (total + added, None)

    residual = lax.scan(forward, jnp.zeros((blk_dev, orbitals, columns), jnp.float32), grouped)[0]
    grad_h = (residual / total_blocks).astype(jnp.bfloat16)
    grad_s = (-(residual * energies) / total_blocks).astype(jnp.bfloat16)

    def backward(carry, item):
        blocks, coeffs, rows = item
        valid = (rows >= 0)[:, None, None]
        safe_rows = jnp.maximum(rows, 0)
        gh_rows = jnp.where(valid, grad_h[safe_rows], jnp.zeros((), jnp.bfloat16))
        gs_rows = jnp.where(valid, grad_s[safe_rows], jnp.zeros((), jnp.bfloat16))
        d_h = jnp.einsum(
            "sap,sbp->sab", gh_rows, coeffs, preferred_element_type=jnp.float32
        ).astype(jnp.bfloat16)
        d_s = jnp.einsum(
            "sap,sbp->sab", gs_rows, coeffs, preferred_element_type=jnp.float32
        ).astype(jnp.bfloat16)
        return (carry, jnp.stack([d_h, d_s], axis=1))

    d_blocks = lax.scan(backward, 0, grouped)[1]
    return (residual, d_blocks.reshape(slots, 2, orbitals, orbitals))


def local(features, w_first, w_second, panel, energies, pair_dest, pair_row, pair_col):
    n_dev = lax.axis_size("blk")
    my_index = lax.axis_index("blk")
    pair_count, feat_width = features.shape
    blk_dev, orbitals, columns = panel.shape
    capacity = 3 * pair_count // (2 * n_dev)
    slots = n_dev * capacity
    total_blocks = blk_dev * n_dev
    dest = pair_dest[:, 0]
    dest_table = (dest[:, None] == jnp.arange(n_dev, dtype=jnp.int32)[None, :]).astype(jnp.int32)
    rank_in = jnp.sum(jnp.cumsum(dest_table, axis=0) * dest_table, axis=1) - 1
    slot_of = dest * capacity + rank_in
    source = (
        jnp.full((slots,), pair_count, jnp.int32)
        .at[slot_of]
        .set(jnp.arange(pair_count, dtype=jnp.int32))
    )
    empty_label = jnp.full((1,), -1, jnp.int32)
    rows_sent = jnp.concatenate([pair_row, empty_label])[source]
    cols_sent = jnp.concatenate([my_index * blk_dev + pair_col, jnp.zeros((1,), jnp.int32)])[source]
    labels = jnp.stack([rows_sent, cols_sent], axis=-1).reshape(n_dev, capacity, 2)
    whole_panel = lax.all_gather(panel, "blk", axis=0, tiled=True)
    pre, hidden, blocks = predict(features, w_first, w_second, orbitals)
    padded = jnp.concatenate([blocks, jnp.zeros((1, blocks.shape[1]), jnp.bfloat16)], axis=0)
    send_blocks = padded[source].reshape(n_dev, capacity, 2, orbitals, orbitals)
    got_blocks, got_labels = (
        lax.all_to_all(send_blocks, "blk", split_axis=0, concat_axis=0, tiled=True),
        lax.all_to_all(labels, "blk", split_axis=0, concat_axis=0, tiled=True),
    )
    got_labels = got_labels.reshape(slots, 2)
    slot_panel = whole_panel[got_labels[:, 1]]
    residual, d_blocks = slot_work(
        got_blocks.reshape(slots, 2, orbitals, orbitals),
        slot_panel,
        got_labels[:, 0],
        energies,
        blk_dev,
        total_blocks,
    )
    back = lax.all_to_all(
        d_blocks.reshape(n_dev, capacity, 2, orbitals, orbitals),
        "blk",
        split_axis=0,
        concat_axis=0,
        tiled=True,
    )
    d_flat = back.reshape(slots, 2 * orbitals * orbitals)[slot_of]
    term_first, term_second = weight_terms(features, pre, hidden, d_flat, w_second, orbitals)
    grad_second = lax.psum_scatter(term_second, "blk", scatter_dimension=1, tiled=True)
    grad_first, square_sum = lax.psum((term_first, jnp.sum(residual * residual)), "blk")
    loss = (square_sum / (total_blocks * orbitals * columns)).reshape(1)
    return (residual, loss, grad_first, grad_second)


def solution(mesh):
    in_specs = (
        P(("parts", "blk"), None),
        P(),
        P(),
        P(("parts", "blk"), None, None),
        P(),
        P(("parts", "blk"), None),
        P(("parts", "blk")),
        P(("parts", "blk")),
    )
    out_specs = (P(("parts", "blk"), None, None), P("parts"), P("parts", None), P("parts", "blk"))
    n_dev = mesh.shape["blk"]
    step = functools.partial(near, z_count=4) if n_dev == 16 else local
    return jax.shard_map(step, mesh=mesh, in_specs=in_specs, out_specs=out_specs, check_vma=False)
```

```python
import functools

import jax
import jax.numpy as jnp
from jax import lax
from jax.experimental import pallas as pl
from jax.experimental.pallas import tpu as pltpu
from jax.sharding import PartitionSpec as P

BF16 = jnp.bfloat16
F32 = jnp.float32
MAIN_VMEM = 50 << 20
W_STEPS = 4
LATE = 9


def dot(a, b, dims):
    return lax.dot_general(a, b, ((dims[:1], dims[1:]), ((), ())), preferred_element_type=F32)


def pack_kernel(dest_ref, row_ref, col_ref, feats_ref, out_ref, *, rs, blk_dev):
    pairs, f_width = feats_ref.shape
    dest = dest_ref[...]
    gid = ((dest % 2) * (2 * rs) + col_ref[...] * rs + (dest // 2) * blk_dev + row_ref[...]).astype(F32)
    out_ref[:pairs, :] = feats_ref[...]
    at = lax.broadcasted_iota(jnp.int32, (8, f_width), 0)
    label = jnp.zeros((8, f_width), F32)
    for k in range(pairs // f_width):
        label = jnp.where(at == k, gid[:, k * f_width : (k + 1) * f_width], label)
    out_ref[pairs:, :] = label.astype(BF16)


def unpack(pack_ref, k, pairs):
    at = k * (pairs + 8)
    f_width = pack_ref.shape[1]
    label = pack_ref[at + pairs : at + pairs + 8, :].astype(F32)
    label = jnp.concatenate([label[q : q + 1, :] for q in range(pairs // f_width)], axis=1)
    return pack_ref[at : at + pairs, :], label


def group_kernel(me_ref, *refs, rs, pairs, orbitals):
    *pack_refs, w_first_ref, mine_ref, theirs_ref, stack_ref = refs
    core = me_ref[0] % 2
    rows = lax.broadcasted_iota(jnp.int32, (4 * rs, pairs), 0)
    rows = ((rows + core * (2 * rs)) % (4 * rs)).astype(F32)
    for k, pack_ref in enumerate(pack_refs):
        feats, label = unpack(pack_ref, 0, pairs)
        pre = dot(feats, w_first_ref[...], (1, 0))
        hidden = (pre * (0.5 * jnp.tanh(0.5 * pre) + 0.5)).astype(BF16)
        pick = (rows == label).astype(F32).astype(BF16)
        sums = (dot(pick, hidden, (1, 0)) * (1.0 / orbitals)).astype(BF16)
        mine_ref[k * 2 * rs : (k + 1) * 2 * rs, :] = sums[: 2 * rs, :]
        theirs_ref[k * 2 * rs : (k + 1) * 2 * rs, :] = sums[2 * rs :, :]
        stack_ref[k * (pairs + 8) : (k + 1) * (pairs + 8), :] = pack_ref[...]


def source_chip(m, chip, chips, z_count):
    x_count = chips // z_count
    return ((chip // x_count - m // x_count) % z_count) * x_count + (chip % x_count - m % x_count) % x_count


def main_kernel(*refs, chips, z_count, rows_split, half_cols, orbitals):
    me_ref, h_refs, p_refs, w_hbm = refs[0], refs[1:5], refs[5:9], refs[9]
    energies_ref, res_ref, keep_ref, send_ref, dh_ref, square_ref = refs[10:16]
    w_ref, w_sems, h_ref, c_ref, x_ref, r_ref, g_ref, l_ref = refs[16:]
    w_steps = w_sems.shape[0]
    step_cols = w_ref.shape[2] // w_steps
    w_copies = []
    for i in range(w_steps):
        cols = slice(i * step_cols, (i + 1) * step_cols)
        w_copies.append(pltpu.make_async_copy(w_hbm.at[:, cols], w_ref.at[0, :, cols], w_sems.at[i]))
        w_copies[i].start()
    me = me_ref[0]
    core = me % 2
    chip = me // 2
    listers = 2 * chips
    rs = rows_split
    half = w_ref.shape[2] // 2
    columns = energies_ref.shape[1]
    ah_count = half // 128
    total_blocks = 2 * rs
    lane = lax.broadcasted_iota(jnp.int32, (rs, 128), 1)
    low = lane < 64

    def place(lister, block):
        at = pl.multiple_of(lister * 128, 128)
        c_ref[0, pl.ds(at, 128), :] = block
        c_ref[1, pl.ds(at, 64), :] = block[64:, :]
        c_ref[1, pl.ds(at + 64, 64), :] = block[:64, :]

    x_count = chips // z_count
    for m in range(chips):
        src = source_chip(m, chip, chips, z_count)
        dz, dx = m // x_count, m % x_count
        for which, lister in ((0, 2 * src + core), (1, 2 * src + 1 - core)):
            place(lister, p_refs[2 * which + dx][dz * 128 : (dz + 1) * 128, :])
            at = pl.multiple_of(lister * rs, rs)
            for pc in range(2):
                lo = dz * 2 * rs + pc * rs
                h_ref[pc, pl.ds(at, rs), :] = h_refs[2 * which + dx][lo : lo + rs, :]

    h0, h1 = h_ref[0], h_ref[1]
    per = step_cols // 128

    for i in range(w_steps):
        at = i * step_cols
        w_copies[i].wait()
        for k in range(per):
            cols = slice(at + k * 128, at + (k + 1) * 128)
            w_ref[1, :, cols] = pltpu.roll(w_ref[0, :, cols].astype(F32), 64, 1).astype(BF16)
        y0 = dot(h0, w_ref[0, :, at : at + step_cols], (1, 0))
        y1 = dot(h1, w_ref[1, :, at : at + step_cols], (1, 0))
        for k in range(per):
            row = (i * per + k) * rs
            for j in range(listers):
                v0 = y0[j * rs : (j + 1) * rs, k * 128 : (k + 1) * 128]
                v1 = y1[j * rs : (j + 1) * rs, k * 128 : (k + 1) * 128]
                cols = slice(j * 128, (j + 1) * 128)
                x_ref[0, row : row + rs, cols] = jnp.where(low, v0, v1).astype(BF16)
                x_ref[1, row : row + rs, cols] = jnp.where(low, v1, v0).astype(BF16)

    energies = energies_ref[...]
    n_rows = ah_count * rs
    mb = 512
    square_ref[...] = jnp.zeros_like(square_ref)

    for i in range(2 * (n_rows // mb)):
        par, b = i // (n_rows // mb), i % (n_rows // mb)
        at = b * mb
        r_h = dot(x_ref[par, pl.ds(at, mb), :], c_ref[par], (1, 0))
        r_s = dot(x_ref[par, pl.ds(n_rows + at, mb), :], c_ref[par], (1, 0))
        res = r_h - r_s * energies
        r_ref[par, pl.ds(at, mb), :] = res
        g_ref[0, par, pl.ds(at, mb), :] = (res / total_blocks).astype(BF16)
        g_ref[1, par, pl.ds(at, mb), :] = (-(res * energies) / total_blocks).astype(BF16)
        square_ref[...] += jnp.sum((res * res).reshape(mb // 8, 8, columns), axis=0)

    blk_dev = res_ref.shape[0]
    for i in range(blk_dev):
        for par in range(2):
            for ah in range(ah_count):
                res_ref[i, 2 * ah + par : 2 * ah + par + 1, :] = r_ref[
                    par, pl.ds(ah * rs + chip * blk_dev + i, 1), :
                ]

    jb_count = 8
    jb_width = jb_count * 128

    for i in range(2 * (listers // jb_count)):
        hs, jb = i // (listers // jb_count), i % (listers // jb_count)
        at = jb * jb_width
        d_e = dot(g_ref[hs, 0], c_ref[0, pl.ds(at, jb_width), :], (1, 1))
        d_o = dot(g_ref[hs, 1], c_ref[1, pl.ds(at, jb_width), :], (1, 1))
        for j in range(jb_count):
            row = (jb * jb_count + j) * rs
            for ah in range(ah_count):
                v0 = d_e[ah * rs : (ah + 1) * rs, j * 128 : (j + 1) * 128]
                v1 = d_o[ah * rs : (ah + 1) * rs, j * 128 : (j + 1) * 128]
                cols = slice(hs * half + ah * 128, hs * half + (ah + 1) * 128)
                l_ref[0, pl.ds(row, rs), cols] = jnp.where(low, v0, v1).astype(BF16)
                l_ref[1, pl.ds(row, rs), cols] = jnp.where(low, v1, v0).astype(BF16)

    for pc in range(2):
        dh_ref[pc] = dot(l_ref[pc], w_ref[pc], (1, 1)) / orbitals

    width = 2 * half_cols
    at = pl.multiple_of(chip * width, width)
    g0 = dot(h0, l_ref[0, :, pl.ds(at, width)], (0, 0))
    g1 = dot(h1, l_ref[1, :, pl.ds(at, width)], (0, 0))
    even = core == 0
    for k in range(half_cols // 128):
        a, b = slice(k * 128, (k + 1) * 128), slice(half_cols + k * 128, half_cols + (k + 1) * 128)
        va = g0[:, a] + pltpu.roll(g1[:, a], 64, 1)
        vb = g0[:, b] + pltpu.roll(g1[:, b], 64, 1)
        keep_ref[:, a] = jnp.where(even, va, vb)
        send_ref[:, a] = jnp.where(even, vb, va)


def first_kernel(*refs, chips, z_count, rs, pairs):
    me_ref, pack_refs = refs[0], refs[1:5]
    w_first_ref, dh_ref, square_ref, first_ref, f_ref, d_ref = refs[5:]
    me = me_ref[0]
    core, chip = me % 2, me // 2
    f_width = w_first_ref.shape[0]
    x_count = chips // z_count
    group_row = (lax.broadcasted_iota(jnp.int32, (2 * rs, pairs), 0) + core * (2 * rs)).astype(F32)
    for m in range(chips):
        src = source_chip(m, chip, chips, z_count)
        dz, dx = m // x_count, m % x_count
        for which, lister in ((0, 2 * src + core), (1, 2 * src + 1 - core)):
            feats, label = unpack(pack_refs[2 * which + dx], dz, pairs)
            pre = dot(feats, w_first_ref[...], (1, 0))
            sig = 0.5 * jnp.tanh(0.5 * pre) + 0.5
            at = pl.multiple_of(lister * rs, rs)
            d_group = jnp.concatenate([dh_ref[0, pl.ds(at, rs), :], dh_ref[1, pl.ds(at, rs), :]], axis=0)
            head = d_group.astype(BF16)
            tail = (d_group - head.astype(F32)).astype(BF16)
            both = jnp.concatenate([head, tail], axis=0)
            pick = (group_row == label).astype(F32).astype(BF16)
            d_hidden = dot(jnp.concatenate([pick, pick], axis=0), both, (0, 0))
            to = pl.multiple_of(lister * pairs, pairs)
            d_ref[pl.ds(to, pairs), :] = (d_hidden * sig * (1.0 + pre * (1.0 - sig))).astype(BF16)
            f_ref[pl.ds(to, pairs), :] = feats
    first_ref[:f_width, :] = dot(f_ref[...], d_ref[...], (0, 0))
    first_ref[f_width:, :] = square_ref[...]


def combine_kernel(keep_ref, sent_ref, first_ref, got_ref, second_ref, grad_ref, loss_ref, *, count):
    second_ref[...] = keep_ref[...] + sent_ref[...]
    f_width = grad_ref.shape[0]
    grad_ref[...] = first_ref[:f_width, :] + got_ref[:f_width, :]
    square = first_ref[f_width:, :] + got_ref[f_width:, :]
    loss_ref[...] = jnp.sum(jnp.sum(square, axis=0, keepdims=True), axis=1, keepdims=True) / count


def near(features, w_first, w_second, panel, energies, pair_dest, pair_row, pair_col, z_count):
    n_dev = lax.axis_size("blk")
    me = lax.axis_index("blk").reshape(1).astype(jnp.int32)
    pairs, f_width = features.shape
    blk_dev, orbitals, columns = panel.shape
    hid, flat = w_second.shape
    chips, rs = n_dev // 2, n_dev * blk_dev // 2
    half_cols = flat // n_dev
    smem, vmem = pl.BlockSpec(memory_space=pltpu.SMEM), pl.BlockSpec(memory_space=pltpu.VMEM)
    anywhere = pl.BlockSpec(memory_space=pl.ANY)
    x_count = chips // z_count

    def to_core(v):
        return lax.ppermute(v, "blk", [(i, i ^ 1) for i in range(n_dev)])

    def from_chip(v, m):
        sends = [(2 * source_chip(m, q, chips, z_count) + c, 2 * q + c) for q in range(chips) for c in range(2)]
        return lax.ppermute(v, "blk", sends) if m else v

    pack = pl.pallas_call(
        functools.partial(pack_kernel, rs=rs, blk_dev=blk_dev),
        out_shape=jax.ShapeDtypeStruct((pairs + 8, f_width), BF16),
        cost_estimate=pl.CostEstimate(flops=0, transcendentals=0, bytes_accessed=1 << 20),
        name="pack",
    )(pair_dest.reshape(1, pairs), pair_row.reshape(1, pairs), pair_col.reshape(1, pairs), features)
    def to_both(v):
        sends = [(2 * source_chip(1, q, chips, z_count) + 1 - c, 2 * q + c) for q in range(chips) for c in range(2)]
        return lax.ppermute(v, "blk", sends)

    rows = panel.reshape(blk_dev * orbitals, columns)
    rows_late, pack = lax.optimization_barrier((rows, pack))
    packs = [from_chip(pack, dz * x_count) for dz in range(z_count)]
    panels_z = [rows] + [from_chip(rows if dz < LATE else rows_late, dz * x_count) for dz in range(1, z_count)]
    panels_z = jnp.concatenate(panels_z, axis=0)
    panels = [panels_z, from_chip(panels_z, 1)]
    h_mine, h_theirs, packs_z = pl.pallas_call(
        functools.partial(group_kernel, rs=rs, pairs=pairs, orbitals=orbitals),
        out_shape=(
            jax.ShapeDtypeStruct((2 * rs * z_count, hid), BF16),
            jax.ShapeDtypeStruct((2 * rs * z_count, hid), BF16),
            jax.ShapeDtypeStruct((z_count * (pairs + 8), f_width), BF16),
        ),
        in_specs=[smem] + [vmem] * (z_count + 1),
        compiler_params=pltpu.CompilerParams(vmem_limit_bytes=12 << 20),
        cost_estimate=pl.CostEstimate(flops=1 << 34, transcendentals=0, bytes_accessed=1 << 21),
        name="group",
    )(me, *packs, w_first)
    hiddens = [h_mine, from_chip(h_mine, 1), to_core(h_theirs), to_both(h_theirs)]
    panels[1], packs_z = lax.optimization_barrier((panels[1], packs_z))
    panels += [to_core(v) for v in panels]
    packs = [packs_z, from_chip(packs_z, 1), to_core(packs_z), to_both(packs_z)]

    listers = n_dev
    k_width = listers * 128
    n_rows = rs * orbitals // 2
    res, keep, send, d_hidden, square = pl.pallas_call(
        functools.partial(
            main_kernel, chips=chips, z_count=z_count, rows_split=rs, half_cols=half_cols, orbitals=orbitals
        ),
        out_shape=(
            jax.ShapeDtypeStruct((blk_dev, orbitals, columns), F32),
            jax.ShapeDtypeStruct((hid, half_cols), F32),
            jax.ShapeDtypeStruct((hid, half_cols), F32),
            jax.ShapeDtypeStruct((2, listers * rs, hid), F32),
            jax.ShapeDtypeStruct((8, columns), F32),
        ),
        in_specs=[smem] + [vmem] * 8 + [anywhere, vmem],
        scratch_shapes=[
            pltpu.VMEM((2, hid, flat), BF16),
            pltpu.SemaphoreType.DMA((W_STEPS,)),
            pltpu.VMEM((2, listers * rs, hid), BF16),
            pltpu.VMEM((2, k_width, columns), BF16),
            pltpu.VMEM((2, 2 * n_rows, k_width), BF16),
            pltpu.VMEM((2, n_rows, columns), F32),
            pltpu.VMEM((2, 2, n_rows, columns), BF16),
            pltpu.VMEM((2, listers * rs, flat), BF16),
        ],
        compiler_params=pltpu.CompilerParams(vmem_limit_bytes=MAIN_VMEM),
        cost_estimate=pl.CostEstimate(flops=1 << 29, transcendentals=0, bytes_accessed=1 << 20),
        name="step",
    )(me, *hiddens, *panels, w_second, energies.reshape(1, columns))
    send = to_core(send)
    first = pl.pallas_call(
        functools.partial(first_kernel, chips=chips, z_count=z_count, rs=rs, pairs=pairs),
        out_shape=jax.ShapeDtypeStruct((f_width + 8, hid), F32),
        in_specs=[smem] + [vmem] * 7,
        scratch_shapes=[pltpu.VMEM((n_dev * pairs, f_width), BF16), pltpu.VMEM((n_dev * pairs, hid), BF16)],
        compiler_params=pltpu.CompilerParams(vmem_limit_bytes=12 << 20),
        cost_estimate=pl.CostEstimate(flops=1 << 31, transcendentals=0, bytes_accessed=1 << 22),
        name="first",
    )(me, *packs, w_first, d_hidden, square)
    count = n_dev * blk_dev * orbitals * columns
    grad_second, grad_first, loss = pl.pallas_call(
        functools.partial(combine_kernel, count=count),
        out_shape=(
            jax.ShapeDtypeStruct((hid, half_cols), F32),
            jax.ShapeDtypeStruct((f_width, hid), F32),
            jax.ShapeDtypeStruct((1, 1), F32),
        ),
        compiler_params=pltpu.CompilerParams(vmem_limit_bytes=12 << 20),
        name="combine",
    )(keep, send, first, to_core(first))
    return (res, loss.reshape(1), grad_first, grad_second)


def predict(feats, w_first, w_second, orbitals):
    pre = jnp.dot(feats, w_first, preferred_element_type=jnp.float32)
    hidden = jax.nn.silu(pre).astype(jnp.bfloat16)
    blocks = (jnp.dot(hidden, w_second, preferred_element_type=jnp.float32) / orbitals).astype(
        jnp.bfloat16
    )
    return (pre, hidden, blocks)


def weight_terms(feats, pre, hidden, d_flat, w_second, orbitals):
    term_second = jnp.dot(hidden.T, d_flat, preferred_element_type=jnp.float32) / orbitals
    d_hidden = (
        lax.dot_general(
            d_flat, w_second, (((1,), (1,)), ((), ())), preferred_element_type=jnp.float32
        )
        / orbitals
    )
    sig = jax.nn.sigmoid(pre)
    d_pre = (d_hidden * sig * (1.0 + pre * (1.0 - sig))).astype(jnp.bfloat16)
    term_first = jnp.dot(feats.T, d_pre, preferred_element_type=jnp.float32)
    return (term_first, term_second)


def slot_work(slot_blocks, slot_panel, slot_rows, energies, blk_dev, total_blocks):
    slots, unused_two, orbitals, unused_o = slot_blocks.shape
    columns = slot_panel.shape[2]
    group = 32
    steps_count = slots // group
    grouped = (
        slot_blocks.reshape(steps_count, group, 2, orbitals, orbitals),
        slot_panel.reshape(steps_count, group, orbitals, columns),
        slot_rows.reshape(steps_count, group),
    )
    row_ids = jnp.arange(blk_dev, dtype=jnp.int32)

    def forward(total, item):
        blocks, coeffs, rows = item
        h_panel = jnp.einsum(
            "sab,sbp->sap", blocks[:, 0], coeffs, preferred_element_type=jnp.float32
        )
        s_panel = jnp.einsum(
            "sab,sbp->sap", blocks[:, 1], coeffs, preferred_element_type=jnp.float32
        )
        contrib = h_panel - s_panel * energies
        selector = (rows[None, :] == row_ids[:, None]).astype(jnp.float32)
        added = jnp.einsum("rs,sap->rap", selector, contrib, precision=lax.Precision.HIGHEST)
        return (total + added, None)

    residual = lax.scan(forward, jnp.zeros((blk_dev, orbitals, columns), jnp.float32), grouped)[0]
    grad_h = (residual / total_blocks).astype(jnp.bfloat16)
    grad_s = (-(residual * energies) / total_blocks).astype(jnp.bfloat16)

    def backward(carry, item):
        blocks, coeffs, rows = item
        valid = (rows >= 0)[:, None, None]
        safe_rows = jnp.maximum(rows, 0)
        gh_rows = jnp.where(valid, grad_h[safe_rows], jnp.zeros((), jnp.bfloat16))
        gs_rows = jnp.where(valid, grad_s[safe_rows], jnp.zeros((), jnp.bfloat16))
        d_h = jnp.einsum(
            "sap,sbp->sab", gh_rows, coeffs, preferred_element_type=jnp.float32
        ).astype(jnp.bfloat16)
        d_s = jnp.einsum(
            "sap,sbp->sab", gs_rows, coeffs, preferred_element_type=jnp.float32
        ).astype(jnp.bfloat16)
        return (carry, jnp.stack([d_h, d_s], axis=1))

    d_blocks = lax.scan(backward, 0, grouped)[1]
    return (residual, d_blocks.reshape(slots, 2, orbitals, orbitals))


def local(features, w_first, w_second, panel, energies, pair_dest, pair_row, pair_col):
    n_dev = lax.axis_size("blk")
    my_index = lax.axis_index("blk")
    pair_count, feat_width = features.shape
    blk_dev, orbitals, columns = panel.shape
    capacity = 3 * pair_count // (2 * n_dev)
    slots = n_dev * capacity
    total_blocks = blk_dev * n_dev
    dest = pair_dest[:, 0]
    dest_table = (dest[:, None] == jnp.arange(n_dev, dtype=jnp.int32)[None, :]).astype(jnp.int32)
    rank_in = jnp.sum(jnp.cumsum(dest_table, axis=0) * dest_table, axis=1) - 1
    slot_of = dest * capacity + rank_in
    source = (
        jnp.full((slots,), pair_count, jnp.int32)
        .at[slot_of]
        .set(jnp.arange(pair_count, dtype=jnp.int32))
    )
    empty_label = jnp.full((1,), -1, jnp.int32)
    rows_sent = jnp.concatenate([pair_row, empty_label])[source]
    cols_sent = jnp.concatenate([my_index * blk_dev + pair_col, jnp.zeros((1,), jnp.int32)])[source]
    labels = jnp.stack([rows_sent, cols_sent], axis=-1).reshape(n_dev, capacity, 2)
    whole_panel = lax.all_gather(panel, "blk", axis=0, tiled=True)
    pre, hidden, blocks = predict(features, w_first, w_second, orbitals)
    padded = jnp.concatenate([blocks, jnp.zeros((1, blocks.shape[1]), jnp.bfloat16)], axis=0)
    send_blocks = padded[source].reshape(n_dev, capacity, 2, orbitals, orbitals)
    got_blocks, got_labels = (
        lax.all_to_all(send_blocks, "blk", split_axis=0, concat_axis=0, tiled=True),
        lax.all_to_all(labels, "blk", split_axis=0, concat_axis=0, tiled=True),
    )
    got_labels = got_labels.reshape(slots, 2)
    slot_panel = whole_panel[got_labels[:, 1]]
    residual, d_blocks = slot_work(
        got_blocks.reshape(slots, 2, orbitals, orbitals),
        slot_panel,
        got_labels[:, 0],
        energies,
        blk_dev,
        total_blocks,
    )
    back = lax.all_to_all(
        d_blocks.reshape(n_dev, capacity, 2, orbitals, orbitals),
        "blk",
        split_axis=0,
        concat_axis=0,
        tiled=True,
    )
    d_flat = back.reshape(slots, 2 * orbitals * orbitals)[slot_of]
    term_first, term_second = weight_terms(features, pre, hidden, d_flat, w_second, orbitals)
    grad_second = lax.psum_scatter(term_second, "blk", scatter_dimension=1, tiled=True)
    grad_first, square_sum = lax.psum((term_first, jnp.sum(residual * residual)), "blk")
    loss = (square_sum / (total_blocks * orbitals * columns)).reshape(1)
    return (residual, loss, grad_first, grad_second)


def solution(mesh):
    in_specs = (
        P(("parts", "blk"), None),
        P(),
        P(),
        P(("parts", "blk"), None, None),
        P(),
        P(("parts", "blk"), None),
        P(("parts", "blk")),
        P(("parts", "blk")),
    )
    out_specs = (P(("parts", "blk"), None, None), P("parts"), P("parts", None), P("parts", "blk"))
    n_dev = mesh.shape["blk"]
    step = functools.partial(near, z_count=4) if n_dev == 16 else local
    return jax.shard_map(step, mesh=mesh, in_specs=in_specs, out_specs=out_specs, check_vma=False)
```

```python
import functools

import jax
import jax.numpy as jnp
from jax import lax
from jax.experimental import pallas as pl
from jax.experimental.pallas import tpu as pltpu
from jax.sharding import PartitionSpec as P

BF16 = jnp.bfloat16
F32 = jnp.float32
MAIN_VMEM = 50 << 20
W_STEPS = 4
LATE = 9


def dot(a, b, dims):
    return lax.dot_general(a, b, ((dims[:1], dims[1:]), ((), ())), preferred_element_type=F32)


def pack_kernel(dest_ref, row_ref, col_ref, feats_ref, out_ref, *, rs, blk_dev):
    pairs, f_width = feats_ref.shape
    dest = dest_ref[...]
    gid = ((dest % 2) * (2 * rs) + col_ref[...] * rs + (dest // 2) * blk_dev + row_ref[...]).astype(F32)
    out_ref[:pairs, :] = feats_ref[...]
    at = lax.broadcasted_iota(jnp.int32, (8, f_width), 0)
    label = jnp.zeros((8, f_width), F32)
    for k in range(pairs // f_width):
        label = jnp.where(at == k, gid[:, k * f_width : (k + 1) * f_width], label)
    out_ref[pairs:, :] = label.astype(BF16)


def unpack(pack_ref, k, pairs):
    at = k * (pairs + 8)
    f_width = pack_ref.shape[1]
    label = pack_ref[at + pairs : at + pairs + 8, :].astype(F32)
    label = jnp.concatenate([label[q : q + 1, :] for q in range(pairs // f_width)], axis=1)
    return pack_ref[at : at + pairs, :], label


def group_kernel(me_ref, *refs, rs, pairs, orbitals):
    *pack_refs, w_first_ref, mine_ref, theirs_ref, stack_ref = refs
    core = me_ref[0] % 2
    rows = lax.broadcasted_iota(jnp.int32, (4 * rs, pairs), 0)
    rows = ((rows + core * (2 * rs)) % (4 * rs)).astype(F32)
    for k, pack_ref in enumerate(pack_refs):
        feats, label = unpack(pack_ref, 0, pairs)
        pre = dot(feats, w_first_ref[...], (1, 0))
        hidden = (pre * (0.5 * jnp.tanh(0.5 * pre) + 0.5)).astype(BF16)
        pick = (rows == label).astype(F32).astype(BF16)
        sums = (dot(pick, hidden, (1, 0)) * (1.0 / orbitals)).astype(BF16)
        mine_ref[k * 2 * rs : (k + 1) * 2 * rs, :] = sums[: 2 * rs, :]
        theirs_ref[k * 2 * rs : (k + 1) * 2 * rs, :] = sums[2 * rs :, :]
        stack_ref[k * (pairs + 8) : (k + 1) * (pairs + 8), :] = pack_ref[...]


def source_chip(m, chip, chips, z_count):
    x_count = chips // z_count
    return ((chip // x_count - m // x_count) % z_count) * x_count + (chip % x_count - m % x_count) % x_count


def main_kernel(*refs, chips, z_count, rows_split, half_cols, orbitals):
    me_ref, h_refs, p_refs, w_hbm = refs[0], refs[1:5], refs[5:9], refs[9]
    energies_ref, res_ref, keep_ref, send_ref, dh_ref, square_ref = refs[10:16]
    w_ref, w_sems, h_ref, c_ref, x_ref, r_ref, g_ref, l_ref = refs[16:]
    w_steps = w_sems.shape[0]
    step_cols = w_ref.shape[2] // w_steps
    w_copies = []
    for i in range(w_steps):
        cols = slice(i * step_cols, (i + 1) * step_cols)
        w_copies.append(pltpu.make_async_copy(w_hbm.at[:, cols], w_ref.at[0, :, cols], w_sems.at[i]))
        w_copies[i].start()
    me = me_ref[0]
    core = me % 2
    chip = me // 2
    listers = 2 * chips
    rs = rows_split
    half = w_ref.shape[2] // 2
    columns = energies_ref.shape[1]
    ah_count = half // 128
    total_blocks = 2 * rs
    lane = lax.broadcasted_iota(jnp.int32, (rs, 128), 1)
    low = lane < 64

    def place(lister, block):
        at = pl.multiple_of(lister * 128, 128)
        c_ref[0, pl.ds(at, 128), :] = block
        c_ref[1, pl.ds(at, 64), :] = block[64:, :]
        c_ref[1, pl.ds(at + 64, 64), :] = block[:64, :]

    x_count = chips // z_count
    for m in range(chips):
        src = source_chip(m, chip, chips, z_count)
        dz, dx = m // x_count, m % x_count
        for which, lister in ((0, 2 * src + core), (1, 2 * src + 1 - core)):
            place(lister, p_refs[2 * which + dx][dz * 128 : (dz + 1) * 128, :])
            at = pl.multiple_of(lister * rs, rs)
            for pc in range(2):
                lo = dz * 2 * rs + pc * rs
                h_ref[pc, pl.ds(at, rs), :] = h_refs[2 * which + dx][lo : lo + rs, :]

    h0, h1 = h_ref[0], h_ref[1]
    per = step_cols // 128

    for i in range(w_steps):
        at = i * step_cols
        w_copies[i].wait()
        for k in range(per):
            cols = slice(at + k * 128, at + (k + 1) * 128)
            w_ref[1, :, cols] = pltpu.roll(w_ref[0, :, cols].astype(F32), 64, 1).astype(BF16)
        y0 = dot(h0, w_ref[0, :, at : at + step_cols], (1, 0))
        y1 = dot(h1, w_ref[1, :, at : at + step_cols], (1, 0))
        for k in range(per):
            row = (i * per + k) * rs
            for j in range(listers):
                v0 = y0[j * rs : (j + 1) * rs, k * 128 : (k + 1) * 128]
                v1 = y1[j * rs : (j + 1) * rs, k * 128 : (k + 1) * 128]
                cols = slice(j * 128, (j + 1) * 128)
                x_ref[0, row : row + rs, cols] = jnp.where(low, v0, v1).astype(BF16)
                x_ref[1, row : row + rs, cols] = jnp.where(low, v1, v0).astype(BF16)

    energies = energies_ref[...]
    n_rows = ah_count * rs
    mb = 256
    square_ref[...] = jnp.zeros_like(square_ref)

    for i in range(2 * (n_rows // mb)):
        par, b = i // (n_rows // mb), i % (n_rows // mb)
        at = b * mb
        r_h = dot(x_ref[par, pl.ds(at, mb), :], c_ref[par], (1, 0))
        r_s = dot(x_ref[par, pl.ds(n_rows + at, mb), :], c_ref[par], (1, 0))
        res = r_h - r_s * energies
        r_ref[par, pl.ds(at, mb), :] = res
        g_ref[0, par, pl.ds(at, mb), :] = (res / total_blocks).astype(BF16)
        g_ref[1, par, pl.ds(at, mb), :] = (-(res * energies) / total_blocks).astype(BF16)
        square_ref[...] += jnp.sum((res * res).reshape(mb // 8, 8, columns), axis=0)

    blk_dev = res_ref.shape[0]
    for i in range(blk_dev):
        for par in range(2):
            for ah in range(ah_count):
                res_ref[i, 2 * ah + par : 2 * ah + par + 1, :] = r_ref[
                    par, pl.ds(ah * rs + chip * blk_dev + i, 1), :
                ]

    jb_count = 8
    jb_width = jb_count * 128

    for i in range(2 * (listers // jb_count)):
        hs, jb = i // (listers // jb_count), i % (listers // jb_count)
        at = jb * jb_width
        d_e = dot(g_ref[hs, 0], c_ref[0, pl.ds(at, jb_width), :], (1, 1))
        d_o = dot(g_ref[hs, 1], c_ref[1, pl.ds(at, jb_width), :], (1, 1))
        for j in range(jb_count):
            row = (jb * jb_count + j) * rs
            for ah in range(ah_count):
                v0 = d_e[ah * rs : (ah + 1) * rs, j * 128 : (j + 1) * 128]
                v1 = d_o[ah * rs : (ah + 1) * rs, j * 128 : (j + 1) * 128]
                cols = slice(hs * half + ah * 128, hs * half + (ah + 1) * 128)
                l_ref[0, pl.ds(row, rs), cols] = jnp.where(low, v0, v1).astype(BF16)
                l_ref[1, pl.ds(row, rs), cols] = jnp.where(low, v1, v0).astype(BF16)

    for pc in range(2):
        dh_ref[pc] = dot(l_ref[pc], w_ref[pc], (1, 1)) / orbitals

    width = 2 * half_cols
    at = pl.multiple_of(chip * width, width)
    g0 = dot(h0, l_ref[0, :, pl.ds(at, width)], (0, 0))
    g1 = dot(h1, l_ref[1, :, pl.ds(at, width)], (0, 0))
    even = core == 0
    for k in range(half_cols // 128):
        a, b = slice(k * 128, (k + 1) * 128), slice(half_cols + k * 128, half_cols + (k + 1) * 128)
        va = g0[:, a] + pltpu.roll(g1[:, a], 64, 1)
        vb = g0[:, b] + pltpu.roll(g1[:, b], 64, 1)
        keep_ref[:, a] = jnp.where(even, va, vb)
        send_ref[:, a] = jnp.where(even, vb, va)


def first_kernel(*refs, chips, z_count, rs, pairs):
    me_ref, pack_refs = refs[0], refs[1:5]
    w_first_ref, dh_ref, square_ref, first_ref, f_ref, d_ref = refs[5:]
    me = me_ref[0]
    core, chip = me % 2, me // 2
    f_width = w_first_ref.shape[0]
    x_count = chips // z_count
    group_row = (lax.broadcasted_iota(jnp.int32, (2 * rs, pairs), 0) + core * (2 * rs)).astype(F32)
    for m in range(chips):
        src = source_chip(m, chip, chips, z_count)
        dz, dx = m // x_count, m % x_count
        for which, lister in ((0, 2 * src + core), (1, 2 * src + 1 - core)):
            feats, label = unpack(pack_refs[2 * which + dx], dz, pairs)
            pre = dot(feats, w_first_ref[...], (1, 0))
            sig = 0.5 * jnp.tanh(0.5 * pre) + 0.5
            at = pl.multiple_of(lister * rs, rs)
            d_group = jnp.concatenate([dh_ref[0, pl.ds(at, rs), :], dh_ref[1, pl.ds(at, rs), :]], axis=0)
            head = d_group.astype(BF16)
            tail = (d_group - head.astype(F32)).astype(BF16)
            both = jnp.concatenate([head, tail], axis=0)
            pick = (group_row == label).astype(F32).astype(BF16)
            d_hidden = dot(jnp.concatenate([pick, pick], axis=0), both, (0, 0))
            to = pl.multiple_of(lister * pairs, pairs)
            d_ref[pl.ds(to, pairs), :] = (d_hidden * sig * (1.0 + pre * (1.0 - sig))).astype(BF16)
            f_ref[pl.ds(to, pairs), :] = feats
    first_ref[:f_width, :] = dot(f_ref[...], d_ref[...], (0, 0))
    first_ref[f_width:, :] = square_ref[...]


def combine_kernel(keep_ref, sent_ref, first_ref, got_ref, second_ref, grad_ref, loss_ref, *, count):
    second_ref[...] = keep_ref[...] + sent_ref[...]
    f_width = grad_ref.shape[0]
    grad_ref[...] = first_ref[:f_width, :] + got_ref[:f_width, :]
    square = first_ref[f_width:, :] + got_ref[f_width:, :]
    loss_ref[...] = jnp.sum(jnp.sum(square, axis=0, keepdims=True), axis=1, keepdims=True) / count


def near(features, w_first, w_second, panel, energies, pair_dest, pair_row, pair_col, z_count):
    n_dev = lax.axis_size("blk")
    me = lax.axis_index("blk").reshape(1).astype(jnp.int32)
    pairs, f_width = features.shape
    blk_dev, orbitals, columns = panel.shape
    hid, flat = w_second.shape
    chips, rs = n_dev // 2, n_dev * blk_dev // 2
    half_cols = flat // n_dev
    smem, vmem = pl.BlockSpec(memory_space=pltpu.SMEM), pl.BlockSpec(memory_space=pltpu.VMEM)
    anywhere = pl.BlockSpec(memory_space=pl.ANY)
    x_count = chips // z_count

    def to_core(v):
        return lax.ppermute(v, "blk", [(i, i ^ 1) for i in range(n_dev)])

    def from_chip(v, m):
        sends = [(2 * source_chip(m, q, chips, z_count) + c, 2 * q + c) for q in range(chips) for c in range(2)]
        return lax.ppermute(v, "blk", sends) if m else v

    pack = pl.pallas_call(
        functools.partial(pack_kernel, rs=rs, blk_dev=blk_dev),
        out_shape=jax.ShapeDtypeStruct((pairs + 8, f_width), BF16),
        cost_estimate=pl.CostEstimate(flops=0, transcendentals=0, bytes_accessed=1 << 20),
        name="pack",
    )(pair_dest.reshape(1, pairs), pair_row.reshape(1, pairs), pair_col.reshape(1, pairs), features)
    def to_both(v):
        sends = [(2 * source_chip(1, q, chips, z_count) + 1 - c, 2 * q + c) for q in range(chips) for c in range(2)]
        return lax.ppermute(v, "blk", sends)

    rows = panel.reshape(blk_dev * orbitals, columns)
    rows_late, pack = lax.optimization_barrier((rows, pack))
    packs = [from_chip(pack, dz * x_count) for dz in range(z_count)]
    panels_z = [rows] + [from_chip(rows if dz < LATE else rows_late, dz * x_count) for dz in range(1, z_count)]
    panels_z = jnp.concatenate(panels_z, axis=0)
    panels = [panels_z, from_chip(panels_z, 1)]
    h_mine, h_theirs, packs_z = pl.pallas_call(
        functools.partial(group_kernel, rs=rs, pairs=pairs, orbitals=orbitals),
        out_shape=(
            jax.ShapeDtypeStruct((2 * rs * z_count, hid), BF16),
            jax.ShapeDtypeStruct((2 * rs * z_count, hid), BF16),
            jax.ShapeDtypeStruct((z_count * (pairs + 8), f_width), BF16),
        ),
        in_specs=[smem] + [vmem] * (z_count + 1),
        compiler_params=pltpu.CompilerParams(vmem_limit_bytes=12 << 20),
        cost_estimate=pl.CostEstimate(flops=1 << 34, transcendentals=0, bytes_accessed=1 << 21),
        name="group",
    )(me, *packs, w_first)
    hiddens = [h_mine, from_chip(h_mine, 1), to_core(h_theirs), to_both(h_theirs)]
    panels[1], packs_z = lax.optimization_barrier((panels[1], packs_z))
    panels += [to_core(v) for v in panels]
    packs = [packs_z, from_chip(packs_z, 1), to_core(packs_z), to_both(packs_z)]

    listers = n_dev
    k_width = listers * 128
    n_rows = rs * orbitals // 2
    res, keep, send, d_hidden, square = pl.pallas_call(
        functools.partial(
            main_kernel, chips=chips, z_count=z_count, rows_split=rs, half_cols=half_cols, orbitals=orbitals
        ),
        out_shape=(
            jax.ShapeDtypeStruct((blk_dev, orbitals, columns), F32),
            jax.ShapeDtypeStruct((hid, half_cols), F32),
            jax.ShapeDtypeStruct((hid, half_cols), F32),
            jax.ShapeDtypeStruct((2, listers * rs, hid), F32),
            jax.ShapeDtypeStruct((8, columns), F32),
        ),
        in_specs=[smem] + [vmem] * 8 + [anywhere, vmem],
        scratch_shapes=[
            pltpu.VMEM((2, hid, flat), BF16),
            pltpu.SemaphoreType.DMA((W_STEPS,)),
            pltpu.VMEM((2, listers * rs, hid), BF16),
            pltpu.VMEM((2, k_width, columns), BF16),
            pltpu.VMEM((2, 2 * n_rows, k_width), BF16),
            pltpu.VMEM((2, n_rows, columns), F32),
            pltpu.VMEM((2, 2, n_rows, columns), BF16),
            pltpu.VMEM((2, listers * rs, flat), BF16),
        ],
        compiler_params=pltpu.CompilerParams(vmem_limit_bytes=MAIN_VMEM),
        cost_estimate=pl.CostEstimate(flops=1 << 29, transcendentals=0, bytes_accessed=1 << 20),
        name="step",
    )(me, *hiddens, *panels, w_second, energies.reshape(1, columns))
    send = to_core(send)
    first = pl.pallas_call(
        functools.partial(first_kernel, chips=chips, z_count=z_count, rs=rs, pairs=pairs),
        out_shape=jax.ShapeDtypeStruct((f_width + 8, hid), F32),
        in_specs=[smem] + [vmem] * 7,
        scratch_shapes=[pltpu.VMEM((n_dev * pairs, f_width), BF16), pltpu.VMEM((n_dev * pairs, hid), BF16)],
        compiler_params=pltpu.CompilerParams(vmem_limit_bytes=12 << 20),
        cost_estimate=pl.CostEstimate(flops=1 << 31, transcendentals=0, bytes_accessed=1 << 22),
        name="first",
    )(me, *packs, w_first, d_hidden, square)
    count = n_dev * blk_dev * orbitals * columns
    grad_second, grad_first, loss = pl.pallas_call(
        functools.partial(combine_kernel, count=count),
        out_shape=(
            jax.ShapeDtypeStruct((hid, half_cols), F32),
            jax.ShapeDtypeStruct((f_width, hid), F32),
            jax.ShapeDtypeStruct((1, 1), F32),
        ),
        compiler_params=pltpu.CompilerParams(vmem_limit_bytes=12 << 20),
        name="combine",
    )(keep, send, first, to_core(first))
    return (res, loss.reshape(1), grad_first, grad_second)


def predict(feats, w_first, w_second, orbitals):
    pre = jnp.dot(feats, w_first, preferred_element_type=jnp.float32)
    hidden = jax.nn.silu(pre).astype(jnp.bfloat16)
    blocks = (jnp.dot(hidden, w_second, preferred_element_type=jnp.float32) / orbitals).astype(
        jnp.bfloat16
    )
    return (pre, hidden, blocks)


def weight_terms(feats, pre, hidden, d_flat, w_second, orbitals):
    term_second = jnp.dot(hidden.T, d_flat, preferred_element_type=jnp.float32) / orbitals
    d_hidden = (
        lax.dot_general(
            d_flat, w_second, (((1,), (1,)), ((), ())), preferred_element_type=jnp.float32
        )
        / orbitals
    )
    sig = jax.nn.sigmoid(pre)
    d_pre = (d_hidden * sig * (1.0 + pre * (1.0 - sig))).astype(jnp.bfloat16)
    term_first = jnp.dot(feats.T, d_pre, preferred_element_type=jnp.float32)
    return (term_first, term_second)


def slot_work(slot_blocks, slot_panel, slot_rows, energies, blk_dev, total_blocks):
    slots, unused_two, orbitals, unused_o = slot_blocks.shape
    columns = slot_panel.shape[2]
    group = 32
    steps_count = slots // group
    grouped = (
        slot_blocks.reshape(steps_count, group, 2, orbitals, orbitals),
        slot_panel.reshape(steps_count, group, orbitals, columns),
        slot_rows.reshape(steps_count, group),
    )
    row_ids = jnp.arange(blk_dev, dtype=jnp.int32)

    def forward(total, item):
        blocks, coeffs, rows = item
        h_panel = jnp.einsum(
            "sab,sbp->sap", blocks[:, 0], coeffs, preferred_element_type=jnp.float32
        )
        s_panel = jnp.einsum(
            "sab,sbp->sap", blocks[:, 1], coeffs, preferred_element_type=jnp.float32
        )
        contrib = h_panel - s_panel * energies
        selector = (rows[None, :] == row_ids[:, None]).astype(jnp.float32)
        added = jnp.einsum("rs,sap->rap", selector, contrib, precision=lax.Precision.HIGHEST)
        return (total + added, None)

    residual = lax.scan(forward, jnp.zeros((blk_dev, orbitals, columns), jnp.float32), grouped)[0]
    grad_h = (residual / total_blocks).astype(jnp.bfloat16)
    grad_s = (-(residual * energies) / total_blocks).astype(jnp.bfloat16)

    def backward(carry, item):
        blocks, coeffs, rows = item
        valid = (rows >= 0)[:, None, None]
        safe_rows = jnp.maximum(rows, 0)
        gh_rows = jnp.where(valid, grad_h[safe_rows], jnp.zeros((), jnp.bfloat16))
        gs_rows = jnp.where(valid, grad_s[safe_rows], jnp.zeros((), jnp.bfloat16))
        d_h = jnp.einsum(
            "sap,sbp->sab", gh_rows, coeffs, preferred_element_type=jnp.float32
        ).astype(jnp.bfloat16)
        d_s = jnp.einsum(
            "sap,sbp->sab", gs_rows, coeffs, preferred_element_type=jnp.float32
        ).astype(jnp.bfloat16)
        return (carry, jnp.stack([d_h, d_s], axis=1))

    d_blocks = lax.scan(backward, 0, grouped)[1]
    return (residual, d_blocks.reshape(slots, 2, orbitals, orbitals))


def local(features, w_first, w_second, panel, energies, pair_dest, pair_row, pair_col):
    n_dev = lax.axis_size("blk")
    my_index = lax.axis_index("blk")
    pair_count, feat_width = features.shape
    blk_dev, orbitals, columns = panel.shape
    capacity = 3 * pair_count // (2 * n_dev)
    slots = n_dev * capacity
    total_blocks = blk_dev * n_dev
    dest = pair_dest[:, 0]
    dest_table = (dest[:, None] == jnp.arange(n_dev, dtype=jnp.int32)[None, :]).astype(jnp.int32)
    rank_in = jnp.sum(jnp.cumsum(dest_table, axis=0) * dest_table, axis=1) - 1
    slot_of = dest * capacity + rank_in
    source = (
        jnp.full((slots,), pair_count, jnp.int32)
        .at[slot_of]
        .set(jnp.arange(pair_count, dtype=jnp.int32))
    )
    empty_label = jnp.full((1,), -1, jnp.int32)
    rows_sent = jnp.concatenate([pair_row, empty_label])[source]
    cols_sent = jnp.concatenate([my_index * blk_dev + pair_col, jnp.zeros((1,), jnp.int32)])[source]
    labels = jnp.stack([rows_sent, cols_sent], axis=-1).reshape(n_dev, capacity, 2)
    whole_panel = lax.all_gather(panel, "blk", axis=0, tiled=True)
    pre, hidden, blocks = predict(features, w_first, w_second, orbitals)
    padded = jnp.concatenate([blocks, jnp.zeros((1, blocks.shape[1]), jnp.bfloat16)], axis=0)
    send_blocks = padded[source].reshape(n_dev, capacity, 2, orbitals, orbitals)
    got_blocks, got_labels = (
        lax.all_to_all(send_blocks, "blk", split_axis=0, concat_axis=0, tiled=True),
        lax.all_to_all(labels, "blk", split_axis=0, concat_axis=0, tiled=True),
    )
    got_labels = got_labels.reshape(slots, 2)
    slot_panel = whole_panel[got_labels[:, 1]]
    residual, d_blocks = slot_work(
        got_blocks.reshape(slots, 2, orbitals, orbitals),
        slot_panel,
        got_labels[:, 0],
        energies,
        blk_dev,
        total_blocks,
    )
    back = lax.all_to_all(
        d_blocks.reshape(n_dev, capacity, 2, orbitals, orbitals),
        "blk",
        split_axis=0,
        concat_axis=0,
        tiled=True,
    )
    d_flat = back.reshape(slots, 2 * orbitals * orbitals)[slot_of]
    term_first, term_second = weight_terms(features, pre, hidden, d_flat, w_second, orbitals)
    grad_second = lax.psum_scatter(term_second, "blk", scatter_dimension=1, tiled=True)
    grad_first, square_sum = lax.psum((term_first, jnp.sum(residual * residual)), "blk")
    loss = (square_sum / (total_blocks * orbitals * columns)).reshape(1)
    return (residual, loss, grad_first, grad_second)


def solution(mesh):
    in_specs = (
        P(("parts", "blk"), None),
        P(),
        P(),
        P(("parts", "blk"), None, None),
        P(),
        P(("parts", "blk"), None),
        P(("parts", "blk")),
        P(("parts", "blk")),
    )
    out_specs = (P(("parts", "blk"), None, None), P("parts"), P("parts", None), P("parts", "blk"))
    n_dev = mesh.shape["blk"]
    step = functools.partial(near, z_count=4) if n_dev == 16 else local
    return jax.shard_map(step, mesh=mesh, in_specs=in_specs, out_specs=out_specs, check_vma=False)
```
